128 devices in a mesh: row: 32 (over x, z, core), col: 4 (over y).
Axes of the slice: x: 4, y: 4, z: 4, core: 2. Of those that a mesh axis runs over, the one named last changes fastest.
Arguments:
- panel: float32 [24576, 1536], P('row', 'col'), as said below
- trailing: float32 [24576, 3072], P('row', 'col'), may hold values from -6 to 6
- child_tiles: float32 [16384, 128, 128], P(('row', 'col')), may hold values from -6 to 6
- child_owner: int32 [16384], P(('row', 'col')), may hold values from 0 to 127, as said below
- child_tile: int32 [16384], P(('row', 'col')), may hold values from 0 to 35
- child_rows: int32 [16384, 128], P(('row', 'col')), may hold values from 0 to 127, each once within a row
Outputs:
- factor_panel: float32 [24576, 1536], P('row', 'col')
- new_trailing: float32 [24576, 3072], P('row', 'col')
The draws below stay inside these ranges and needn't reach their ends.
Inputs may be any that keep to these rules, and one draw needn't show every extreme that they name: `panel`: the symmetric part of the first 1536 rows is positive definite. `child_owner`: the 128 tiles of one device name every owner at most 2 times; one owner, drawn from the seed, is named exactly 2 times by every device.
All inputs are finite; a program needn't handle non-finite values.
Results may differ from the reference program's by a relative error of at most 0.000057.
Values sent between devices are 32-bit elements; how exact they have to be, the bound alone decides.
A program may use at most 256 MiB of HBM per device.

```python
import math
import jax
import jax.numpy as jnp
from jax import lax

F = 24576
PW = 1536
TB = 128
TCD = 768
CH = 128
RD = 768
TW = 3072
TPO = 36
CHILDREN = 16384
CAP = 2
N_COL = 4
DEVICES = 128


def draw_panel(key, part):
    values = jax.random.normal(key, (F, PW), jnp.float32)
    row_ids = jnp.arange(F, dtype=jnp.int32)[:, None]
    col_ids = jnp.arange(PW, dtype=jnp.int32)[None, :]
    shift = 3.0 * math.sqrt(PW)
    return values + jnp.where(row_ids == col_ids, shift, 0.0).astype(jnp.float32)


def draw_child_owner(key, part):
    hot_owner = jax.random.randint(jax.random.fold_in(key, 7), (), 0, DEVICES).astype(jnp.int32)
    owner_pool = jnp.arange((DEVICES - 1) * CAP, dtype=jnp.int32) // CAP
    owner_pool = owner_pool + (owner_pool >= hot_owner).astype(jnp.int32)

    def one_sender(sender):
        sender_key = jax.random.fold_in(jax.random.fold_in(key, 11), sender)
        first_key, second_key = jax.random.split(sender_key)
        chosen = jax.random.permutation(first_key, owner_pool)[:CH - CAP]
        filled = jnp.concatenate([jnp.full((CAP,), hot_owner, jnp.int32), chosen])
        return jax.random.permutation(second_key, filled)
    return jax.vmap(one_sender)(jnp.arange(DEVICES, dtype=jnp.int32)).reshape(-1).astype(jnp.int32)


def set_ends(entries, key, least, top_value):
    longest = entries.shape.index(max(entries.shape))
    spots = []
    for shift in (0, 1):
        where = [jax.random.randint(jax.random.fold_in(key, axis), (), 0, length) for axis, length in enumerate(entries.shape)]
        where[longest] = (where[longest] + shift) % entries.shape[longest]
        spots.append(tuple(where))
    return entries.at[spots[0]].set(least).at[spots[1]].set(top_value)


def shard_levels(rng, extent, cuts, least, largest):
    def one(dim, blocks):
        steps = jax.random.uniform(jax.random.fold_in(jax.random.fold_in(rng, 6), dim), (blocks,), jnp.float32, least / len(cuts), largest / len(cuts))
        return jnp.repeat(jnp.exp(steps), extent[dim] // blocks).reshape((-1,) + (1,) * (len(extent) - dim - 1))

    loudness = one(*cuts[0])
    for cut in cuts[1:]:
        loudness = loudness * one(*cut)
    return loudness


def normal_values(key, extent, width, bound, cuts=(), kind=jnp.bfloat16):
    array = jax.random.normal(key, extent, jnp.float32) * width
    if len(cuts) > 0:
        array = shard_levels(key, extent, cuts, -0.22, 0.18) * array
    return jnp.clip(array, min=-bound, max=bound).astype(kind)


def setup_inputs(seed: int = 0) -> dict:
    splits = jax.random.split(jax.random.key(seed), 7)
    return {
        "panel": draw_panel(jax.random.fold_in(splits[6], 71), 0),
        "trailing": normal_values(splits[1], (F, TW), 1.0, 6.0, ((0, 32), (1, 4)), jnp.float32),
        "child_tiles": normal_values(splits[2], (CHILDREN, TB, TB), 1.0, 6.0, ((0, 128),), jnp.float32),
        "child_owner": draw_child_owner(jax.random.fold_in(splits[6], 71), 0),
        "child_tile": set_ends(jax.random.randint(splits[4], (CHILDREN,), 0, TPO), jax.random.fold_in(splits[4], 1), 0, TPO - 1).astype(jnp.int32),
        "child_rows": jax.vmap(lambda own: jax.random.permutation(own, TB))(jax.random.split(splits[5], CHILDREN)).reshape((CHILDREN, TB)).astype(jnp.int32),
    }


def reference(panel, trailing, child_tiles, child_owner, child_tile, child_rows):
    owner_row = child_owner // N_COL
    owner_col = child_owner % N_COL
    tile_cols = TCD // TB
    global_tile_row = (owner_row * (RD // TB) + child_tile // tile_cols).astype(jnp.int32)
    global_tile_col = (owner_col * tile_cols + child_tile % tile_cols).astype(jnp.int32)
    blocked = trailing.reshape(F // TB, TB, TW // TB, TB)
    blocked = blocked.at[global_tile_row[:, None], child_rows, global_tile_col[:, None]].add(child_tiles)
    assembled = blocked.reshape(F, TW)
    diagonal_factor = jnp.linalg.cholesky(panel[:PW])
    solved = jax.scipy.linalg.solve_triangular(diagonal_factor, panel.T, lower=True).T
    factor_panel = solved.at[:PW].set(diagonal_factor)
    column_factor = factor_panel[PW:PW + TW]
    product = lax.dot_general(factor_panel[PW:], column_factor, (((1,), (1,)), ((), ())), precision=lax.Precision.HIGHEST)
    new_trailing = assembled.at[PW:].add(-product)
    return (factor_panel, new_trailing)
```

```python
import jax
import jax.numpy as jnp
from jax import lax
from jax.experimental import pallas as pl
from jax.experimental.pallas import tpu as pltpu
from jax.sharding import PartitionSpec as P

PW = 1536
NB = 128
KB = PW // NB
TB = 128
MESH = pl.DeviceIdType.MESH
F32 = jnp.float32
BF16 = jnp.bfloat16
BIG = 60 << 20


def dot_nt(a, b):
    return lax.dot_general(
        a, b, (((1,), (1,)), ((), ())),
        precision=lax.Precision.HIGHEST, preferred_element_type=F32)


def dot_b(a, b):
    return lax.dot_general(a, b, (((1,), (1,)), ((), ())), preferred_element_type=F32)


def split2(v):
    hi = v.astype(BF16)
    return hi, (v - hi.astype(F32)).astype(BF16)


def dot3(ah, al, bh, bl):
    return dot_b(ah, bh) + (dot_b(ah, bl) + dot_b(al, bh))


def pack_kernel(dst_ref, tiles_ref, rows_ref, out_ref, stage, sems):
    step = pl.program_id(0)
    steps = pl.num_programs(0)
    slot = lax.rem(step, 2)
    per = tiles_ref.shape[0]

    def copy(at, i, which):
        return pltpu.make_async_copy(
            stage.at[which, i], out_ref.at[dst_ref[at * per + i]], sems.at[which, i])

    @pl.when(step >= 2)
    def _():
        for i in range(per):
            copy(step - 2, i, slot).wait()

    sub = lax.broadcasted_iota(jnp.int32, (TB, TB), 0)
    for i in range(per):
        pick = jnp.where(sub == rows_ref[i:i + 1, :], 1.0, 0.0).astype(BF16)
        tile = tiles_ref[i]
        hi = tile.astype(BF16)
        rest = tile - hi.astype(F32)
        mid = rest.astype(BF16)
        low = (rest - mid.astype(F32)).astype(BF16)
        moved = jnp.dot(pick, hi, preferred_element_type=F32)
        moved = moved + jnp.dot(pick, mid, preferred_element_type=F32)
        moved = moved + jnp.dot(pick, low, preferred_element_type=F32)
        stage[slot, i] = moved
    for i in range(per):
        copy(step, i, slot).start()

    @pl.when(step == steps - 1)
    def _():
        for i in range(per):
            copy(step - 1, i, 1 - slot).wait()
        for i in range(per):
            copy(step, i, slot).wait()


def pack(dst, tiles, rows, slots):
    count = tiles.shape[0]
    per = 8
    return pl.pallas_call(
        pack_kernel,
        grid_spec=pltpu.PrefetchScalarGridSpec(
            num_scalar_prefetch=1,
            grid=(count // per,),
            in_specs=[
                pl.BlockSpec((per, TB, TB), lambda i, d: (i, 0, 0)),
                pl.BlockSpec((per, TB), lambda i, d: (i, 0)),
            ],
            out_specs=pl.BlockSpec(memory_space=pl.ANY),
            scratch_shapes=[
                pltpu.VMEM((2, per, TB, TB), F32),
                pltpu.SemaphoreType.DMA((2, per)),
            ],
        ),
        out_shape=jax.ShapeDtypeStruct((slots, TB, TB), F32),
        name="pack",
    )(dst, tiles, rows)


def bcast_kernel(pa_ref, pc_ref, ga_ref, gc_ref,
                 s1a, s1c, r1a, r1c, loc, ss, rs, fs, fr, xs, xr):
    row = lax.axis_index("row")
    y = lax.axis_index("col")
    core = lax.rem(row, 2)
    z = lax.rem(lax.div(row, 2), 4)
    x = lax.div(row, 8)
    xz = lax.div(row, 2)
    pos = {"x": x, "y": y, "z": z}

    def device(axis, p):
        q = dict(pos)
        q[axis] = p
        return ((q["x"] * 4 + q["z"]) * 2 + core, q["y"])

    def remote(src, dst, send, recv, dev):
        return pltpu.make_async_remote_copy(
            src_ref=src, dst_ref=dst, send_sem=send, recv_sem=recv,
            device_id=dev, device_id_type=MESH)

    def piece_a(q):
        return pa_ref.at[:, q], ga_ref.at[:, y, core, lax.div(q, 4), lax.rem(q, 4)]

    def send_a(q):
        s, d = piece_a(q)
        return remote(s, d, s1a.at[q], r1a.at[0], (q * 2 + core, y))

    to_col = row - 2
    to_core = lax.div(y, 2)

    def piece_c(q):
        return pc_ref.at[q], gc_ref.at[y, lax.div(q, 4), lax.rem(q, 4)]

    def send_c(q):
        s, d = piece_c(q)
        return remote(s, d, s1c.at[q], r1c.at[lax.rem(y, 2)], (q * 2 + to_core, to_col))

    is_a = row < 2
    is_c = (row >= 2) & (row < 6)

    @pl.when(is_a)
    def _():
        s, d = piece_a(0)
        pltpu.make_async_copy(s, d, loc.at[0]).start()

        @pl.loop(1, 16)
        def _(q):
            send_a(q).start()

    def keeps(q):
        return (q == xz) & (to_core == core) & (to_col == y)

    @pl.when(is_c)
    def _():
        @pl.loop(0, 16)
        def _(q):
            @pl.when(keeps(q))
            def _():
                s, d = piece_c(q)
                pltpu.make_async_copy(s, d, loc.at[1]).start()

            @pl.when(jnp.logical_not(keeps(q)))
            def _():
                send_c(q).start()

    @pl.when(is_a)
    def _():
        s, d = piece_a(0)
        pltpu.make_async_copy(s, d, loc.at[0]).wait()

    @pl.when(jnp.logical_not(is_a))
    def _():
        s = pa_ref.at[:, 0]
        remote(s, ga_ref.at[:, y, core, x, z], s1a.at[0], r1a.at[0], (row, y)).wait_recv()

    for h in range(2):
        yy = 2 * core + h
        mine = (yy == y) & (row == y + 2)

        @pl.when(mine)
        def _():
            s, d = piece_c(xz)
            pltpu.make_async_copy(s, d, loc.at[1]).wait()

        @pl.when(jnp.logical_not(mine))
        def _():
            remote(pc_ref.at[0], gc_ref.at[yy, x, z], s1c.at[0], r1c.at[h], (row, y)).wait_recv()

    chains = []
    for s, order in enumerate((("z", "x", "y"), ("x", "y", "z"), ("y", "z", "x"))):
        chains.append(("a", s, order))
    for s, order in enumerate((("z", "x"), ("x", "z"))):
        chains.append(("c", s, order))

    def block(kind, s, order, t, p, half=None):
        ind = {}
        for j, a in enumerate(order):
            ind[a] = slice(None) if j < t else (p if j == t else pos[a])
        if kind == "a":
            tail = () if half is None else (pl.ds(8 * half, 8), slice(None))
            fill = () if half is None else tail
            return ga_ref.at[(s, ind["y"], core, ind["x"], ind["z"]) + fill]
        fill = () if half is None else (pl.ds(24 * half, 24), slice(None))
        return gc_ref.at[(2 * core + s, ind["x"], ind["z"]) + fill]

    sibling = (xz * 2 + (1 - core), y)

    def near(n, t, up):
        kind, s, order = chains[n]
        a = order[t]
        p = pos[a]
        b = block(kind, s, order, t, p)
        return remote(b, b, ss.at[n, t, up], rs.at[n, t, up],
                      device(a, lax.rem(p + (1 if up else 3), 4)))

    def near_wait(n, t, up):
        kind, s, order = chains[n]
        a = order[t]
        b = block(kind, s, order, t, lax.rem(pos[a] + (3 if up else 1), 4))
        remote(b, b, ss.at[n, t, up], rs.at[n, t, up], (row, y)).wait_recv()

    def far(n, t, up):
        kind, s, order = chains[n]
        a = order[t]
        p = pos[a]
        b = block(kind, s, order, t, lax.rem(p + (3 if up else 1), 4), 0 if up else 1)
        return remote(b, b, fs.at[n, t, up], fr.at[n, t, up],
                      device(a, lax.rem(p + (1 if up else 3), 4)))

    def far_wait(n, t, up):
        kind, s, order = chains[n]
        a = order[t]
        b = block(kind, s, order, t, lax.rem(pos[a] + 2, 4), 0 if up else 1)
        remote(b, b, fs.at[n, t, up], fr.at[n, t, up], (row, y)).wait_recv()

    def cross(n, shift):
        kind, s, order = chains[n]
        t = len(order) - 1
        b = block(kind, s, order, t, lax.rem(pos[order[t]] + shift, 4))
        return remote(b, b, xs.at[n, shift], xr.at[n, shift], sibling)

    def cross_wait(n, shift):
        kind, s, order = chains[n]
        t = len(order) - 1
        ind = {}
        for j, a in enumerate(order):
            ind[a] = slice(None) if j < t else lax.rem(pos[a] + shift, 4)
        if kind == "a":
            b = ga_ref.at[s, ind["y"], 1 - core, ind["x"], ind["z"]]
        else:
            b = gc_ref.at[2 * (1 - core) + s, ind["x"], ind["z"]]
        remote(b, b, xs.at[n, shift], xr.at[n, shift], (row, y)).wait_recv()

    for t in range(3):
        live = [n for n in range(5) if t < len(chains[n][2])]
        last = [n for n in live if t == len(chains[n][2]) - 1]
        for n in live:
            for up in range(2):
                near(n, t, up).start()
        for n in last:
            cross(n, 0).start()
        for n in live:
            for up in range(2):
                near_wait(n, t, up)
                far(n, t, up).start()
                if n in last:
                    cross(n, 3 if up else 1).start()
        for n in live:
            for up in range(2):
                far_wait(n, t, up)
        for n in last:
            cross(n, 2).start()
    for n in range(5):
        for shift in range(4):
            cross_wait(n, shift)
    for n in range(5):
        for t in range(len(chains[n][2])):
            for up in range(2):
                near(n, t, up).wait_send()
                far(n, t, up).wait_send()
        for shift in range(4):
            cross(n, shift).wait_send()

    @pl.when(is_a)
    def _():
        @pl.loop(1, 16)
        def _(q):
            send_a(q).wait_send()

    @pl.when(is_c)
    def _():
        @pl.loop(0, 16)
        def _(q):
            @pl.when(jnp.logical_not(keeps(q)))
            def _():
                send_c(q).wait_send()


def bcast(panel):
    rows, cols = panel.shape
    dma = pltpu.SemaphoreType.DMA
    return pl.pallas_call(
        bcast_kernel,
        in_specs=[pl.BlockSpec(memory_space=pl.ANY)] * 2,
        out_specs=[pl.BlockSpec(memory_space=pl.ANY)] * 2,
        out_shape=[
            jax.ShapeDtypeStruct((3, 4, 2, 4, 4, 16, cols), F32),
            jax.ShapeDtypeStruct((4, 4, 4, 48, cols), F32),
        ],
        scratch_shapes=[
            dma((16,)), dma((16,)), dma((1,)), dma((2,)), dma((2,)),
            dma((5, 3, 2)), dma((5, 3, 2)), dma((5, 3, 2)), dma((5, 3, 2)),
            dma((5, 4)), dma((5, 4)),
        ],
        compiler_params=pltpu.CompilerParams(has_side_effects=True),
        name="bcast",
    )(panel.reshape(3, 16, 16, cols), panel.reshape(16, 48, cols))


def wide(v):
    return jnp.broadcast_to(v, (8, 128))


def small_inverse(cols):
    c = [[None] * 8 for _ in range(8)]
    for j in range(8):
        for i in range(j, 8):
            c[i][j] = wide(cols[j][i:i + 1, :])
    t = [[None] * 8 for _ in range(8)]
    for j in range(8):
        r = lax.rsqrt(c[j][j])
        t[j][j] = r
        for i in range(j + 1, 8):
            c[i][j] = c[i][j] * r
        for m in range(j + 1, 8):
            for i in range(m, 8):
                c[i][m] = c[i][m] - c[i][j] * c[m][j]
        for k in range(j):
            s = c[j][k] * t[k][k]
            for m in range(k + 1, j):
                s = s + c[j][m] * t[m][k]
            t[j][k] = -(s * r)
    return t


def factor_block(d):
    row = lax.broadcasted_iota(jnp.int32, (NB, NB), 0)
    col = lax.broadcasted_iota(jnp.int32, (NB, NB), 1)
    eye = jnp.where(row == col, 1.0, 0.0).astype(F32)
    groups = NB // 8
    r = [d[8 * g:8 * g + 8, :] for g in range(groups)]
    w = [eye[8 * g:8 * g + 8, :] for g in range(groups)]
    sub = lax.broadcasted_iota(jnp.int32, (8, NB), 0)
    us, vs = [], []
    for g in range(groups):
        cols = [wide(r[g][:, 8 * g + j:8 * g + j + 1]) for j in range(8)]
        t = small_inverse(cols)
        u = v = None
        for j in range(8):
            part = jnp.zeros((8, NB), F32)
            for i in range(j, 8):
                part = jnp.where(sub == i, t[i][j], part)
            du, dv = part * r[g][j:j + 1, :], part * w[g][j:j + 1, :]
            u, v = (du, dv) if u is None else (u + du, v + dv)
        us.append(u)
        vs.append(v)
        if g + 1 < groups:
            nxt = [wide(r[g + 1][:, 8 * g + j:8 * g + j + 1]) for j in range(8)]
            ra, wa = r[g + 1], w[g + 1]
            for j in range(8):
                m = nxt[0] * t[j][0]
                for k in range(1, j + 1):
                    m = m + nxt[k] * t[j][k]
                ra = ra - m * u[j:j + 1, :]
                wa = wa - m * v[j:j + 1, :]
            r[g + 1], w[g + 1] = ra, wa
        if g + 2 < groups:
            ut = jnp.transpose(u)
            for g2 in range(g + 2, groups):
                blk = ut[8 * g2:8 * g2 + 8, :]
                ra, wa = r[g2], w[g2]
                for j in range(8):
                    m = wide(blk[:, j:j + 1])
                    ra = ra - m * u[j:j + 1, :]
                    wa = wa - m * v[j:j + 1, :]
                r[g2], w[g2] = ra, wa
    upper = jnp.concatenate(us, axis=0)
    inverse = jnp.concatenate(vs, axis=0)
    return jnp.where(col >= row, upper, 0.0), inverse


def chol_kernel(ga_ref, l_ref, w_ref, c_ref):
    def given(i, j):
        r, c = i * NB, j * NB
        a, b = r % 256, c % 384
        return ga_ref[(r % 768) // 256, c // 384, r // 768, a:a + NB, b:b + NB]

    def sym(i, j):
        return 0.5 * (given(i, j) + given(j, i).T)

    def at(i):
        return slice(i * NB, (i + 1) * NB)

    d = sym(0, 0)
    last_w = None
    for k in range(KB):
        done = slice(0, k * NB)
        below = slice((k + 1) * NB, PW)
        rest = None
        if k + 1 < KB:
            if k > 0:
                l_ref[below, at(k - 1)] = dot_nt(c_ref[below, :], last_w)
                acc = dot_nt(l_ref[below, done], l_ref[at(k), done])
                for i in range(k + 1, KB):
                    c_ref[at(i), :] = sym(i, k) - acc[at(i - k - 1), :]
                nxt = l_ref[at(k + 1), done]
                rest = sym(k + 1, k + 1) - dot_nt(nxt, nxt)
            else:
                for i in range(1, KB):
                    c_ref[at(i), :] = sym(i, 0)
                rest = sym(1, 1)
        upper, inverse = factor_block(d)
        l_ref[at(k), at(k)] = upper.T
        w_ref[at(k), :] = inverse
        if k + 1 < KB:
            l_ref[at(k), below] = jnp.zeros((NB, PW - (k + 1) * NB), F32)
            nxt = dot_nt(c_ref[at(k + 1), :], inverse)
            l_ref[at(k + 1), at(k)] = nxt
            d = rest - dot_nt(nxt, nxt)
            last_w = inverse


def chol(ga):
    return pl.pallas_call(
        chol_kernel,
        out_shape=[
            jax.ShapeDtypeStruct((PW, PW), F32),
            jax.ShapeDtypeStruct((PW, NB), F32),
        ],
        scratch_shapes=[pltpu.VMEM((PW, NB), F32)],
        compiler_params=pltpu.CompilerParams(vmem_limit_bytes=BIG),
        cost_estimate=pl.CostEstimate(
            flops=60_000_000_000, bytes_accessed=20_000_000, transcendentals=0),
        name="chol",
    )(ga)


def solve_kernel(place_ref, l_ref, w_ref, pr_ref, pc_ref, t_ref, f_ref, o_ref,
                 lh, ll, wh, wl, xh, xl, keep):
    row = place_ref[0]
    col = place_ref[1]
    rows = pr_ref.shape[1]
    wide_cols = pr_ref.shape[2]
    nb = 2 * NB

    @pl.loop(0, KB)
    def _(k):
        at = pl.ds(pl.multiple_of(k * NB, NB), NB)
        hi, lo = split2(l_ref[at, :])
        lh[at, :] = hi
        ll[at, :] = lo

    for k in range(KB // 2):
        a, b = 2 * k * NB, (2 * k + 1) * NB
        w1, w2 = w_ref[a:a + NB, :], w_ref[b:b + NB, :]
        cross = l_ref[b:b + NB, a:a + NB]
        mid = jnp.dot(cross, w1, precision=lax.Precision.HIGHEST, preferred_element_type=F32)
        low = -jnp.dot(w2, mid, precision=lax.Precision.HIGHEST, preferred_element_type=F32)
        zero = jnp.zeros((NB, NB), F32)
        hi, lo = split2(jnp.concatenate(
            [jnp.concatenate([w1, zero], axis=1), jnp.concatenate([low, w2], axis=1)], axis=0))
        wh[k] = hi
        wl[k] = lo

    for part, src in enumerate((pr_ref, pc_ref)):
        for k in range(KB // 2):
            cols = []
            for j in range(2):
                at = (2 * k + j) * NB
                cols.append(src[at // wide_cols, :, at % wide_cols:at % wide_cols + NB])
            v = jnp.concatenate(cols, axis=1)
            if k > 0:
                done = slice(0, k * nb)
                here = slice(k * nb, (k + 1) * nb)
                v = v - dot3(xh[part, :, done], xl[part, :, done], lh[here, done], ll[here, done])
            vh, vl = split2(v)
            v = dot3(vh, vl, wh[k], wl[k])
            hi, lo = split2(v)
            here = slice(k * nb, (k + 1) * nb)
            xh[part, :, here] = hi
            xl[part, :, here] = lo
            if part == 0:
                for j in range(2):
                    at = (2 * k + j) * NB
                    keep[at // wide_cols, :, at % wide_cols:at % wide_cols + NB] = (
                        v[:, j * NB:(j + 1) * NB])

    @pl.when(row >= 2)
    def _():
        f_ref[...] = keep[col]
        for i in range(rows // 256):
            at = slice(i * 256, (i + 1) * 256)
            o_ref[at, :] = t_ref[at, :] - dot3(xh[0, at, :], xl[0, at, :], xh[1], xl[1])

    @pl.when(row < 2)
    def _():
        first = pl.ds(pl.multiple_of(row * rows, NB), rows)
        f_ref[...] = l_ref[first, pl.ds(pl.multiple_of(col * wide_cols, NB), wide_cols)]
        o_ref[...] = t_ref[...]


def solve(place, factor, inverse, mine, theirs, trailing):
    n, rows, cols = mine.shape
    smem = pl.BlockSpec(memory_space=pltpu.SMEM)
    vmem = pl.BlockSpec(memory_space=pltpu.VMEM)
    return pl.pallas_call(
        solve_kernel,
        in_specs=[smem] + [vmem] * 5,
        out_specs=[vmem, vmem],
        out_shape=[
            jax.ShapeDtypeStruct((rows, cols), F32),
            jax.ShapeDtypeStruct(trailing.shape, F32),
        ],
        scratch_shapes=[
            pltpu.VMEM((PW, PW), BF16), pltpu.VMEM((PW, PW), BF16),
            pltpu.VMEM((KB // 2, 2 * NB, 2 * NB), BF16), pltpu.VMEM((KB // 2, 2 * NB, 2 * NB), BF16),
            pltpu.VMEM((2, rows, PW), BF16), pltpu.VMEM((2, rows, PW), BF16),
            pltpu.VMEM((n, rows, cols), F32),
        ],
        compiler_params=pltpu.CompilerParams(vmem_limit_bytes=BIG),
        cost_estimate=pl.CostEstimate(
            flops=30_000_000_000, bytes_accessed=30_000_000, transcendentals=0),
        name="solve",
    )(place, factor, inverse, mine, theirs, trailing)


def add_kernel(target_ref, tiles_ref, base_ref, out_ref):
    step = pl.program_id(0)
    per = tiles_ref.shape[0]
    tile_cols = out_ref.shape[1] // TB

    @pl.when(step == 0)
    def _():
        out_ref[...] = base_ref[...]

    for i in range(per):
        target = target_ref[step * per + i]

        @pl.when(target >= 0)
        def _():
            r = pl.ds(pl.multiple_of(lax.div(target, tile_cols) * TB, TB), TB)
            c = pl.ds(pl.multiple_of(lax.rem(target, tile_cols) * TB, TB), TB)
            out_ref[r, c] = out_ref[r, c] + tiles_ref[i]


def extend_add(target, tiles, base):
    per = 16
    return pl.pallas_call(
        add_kernel,
        grid_spec=pltpu.PrefetchScalarGridSpec(
            num_scalar_prefetch=1,
            grid=(tiles.shape[0] // per,),
            in_specs=[
                pl.BlockSpec((per, TB, TB), lambda i, t: (i, 0, 0)),
                pl.BlockSpec(base.shape, lambda i, t: (0, 0)),
            ],
            out_specs=pl.BlockSpec(base.shape, lambda i, t: (0, 0)),
        ),
        out_shape=jax.ShapeDtypeStruct(base.shape, F32),
        compiler_params=pltpu.CompilerParams(vmem_limit_bytes=32 << 20),
        name="extend_add",
    )(target, tiles, base)


def body(panel, trailing, child_tiles, child_owner, child_tile, child_rows):
    devices = lax.axis_size("row") * lax.axis_size("col")
    count = child_owner.shape[0]
    cap = 2
    both = ("row", "col")
    order = jnp.arange(count, dtype=jnp.int32)
    same = child_owner[:, None] == child_owner[None, :]
    rank = jnp.sum(jnp.where(same & (order[None, :] < order[:, None]), 1, 0), axis=1)
    dst = (child_owner * cap + rank).astype(jnp.int32)
    slots = devices * cap
    hit = dst[:, None] == jnp.arange(slots, dtype=jnp.int32)[None, :]
    target = (jnp.sum(jnp.where(hit, child_tile[:, None] + 1, 0), axis=0) - 1).astype(jnp.int32)
    got_target = lax.all_to_all(
        target.reshape(devices, cap), both, split_axis=0, concat_axis=0, tiled=True)
    packed = pack(dst, child_tiles, child_rows, slots)
    got = lax.all_to_all(
        packed.reshape(devices, cap, TB, TB), both, split_axis=0, concat_axis=0, tiled=True)

    mine = lax.all_gather(panel, "col", axis=0)
    ga, gc = bcast(panel)
    factor, inverse = chol(ga.reshape(3, 4, 2, 256, panel.shape[1]))
    place = jnp.stack([lax.axis_index("row"), lax.axis_index("col")]).astype(jnp.int32)
    factor_panel, base = solve(
        place, factor, inverse, mine, gc.reshape(4, panel.shape[0], panel.shape[1]), trailing)
    new_trailing = extend_add(got_target.reshape(-1), got.reshape(-1, TB, TB), base)
    return factor_panel, new_trailing


def solution(mesh):
    in_specs = (
        P("row", "col"),
        P("row", "col"),
        P(("row", "col"), None, None),
        P(("row", "col")),
        P(("row", "col")),
        P(("row", "col"), None),
    )
    out_specs = (P("row", "col"), P("row", "col"))
    return jax.shard_map(body, mesh=mesh, in_specs=in_specs, out_specs=out_specs, check_vma=False)
```

```python
import jax
import jax.numpy as jnp
from jax import lax
from jax.experimental import pallas as pl
from jax.experimental.pallas import tpu as pltpu
from jax.sharding import PartitionSpec as P

PW = 1536
NB = 128
KB = PW // NB
TB = 128
MESH = pl.DeviceIdType.MESH
F32 = jnp.float32
BF16 = jnp.bfloat16
BIG = 60 << 20


def dot_nt(a, b):
    return lax.dot_general(
        a, b, (((1,), (1,)), ((), ())),
        precision=lax.Precision.HIGHEST, preferred_element_type=F32)


def dot_b(a, b):
    return lax.dot_general(a, b, (((1,), (1,)), ((), ())), preferred_element_type=F32)


def split2(v):
    hi = v.astype(BF16)
    return hi, (v - hi.astype(F32)).astype(BF16)


def dot3(ah, al, bh, bl):
    return dot_b(ah, bh) + (dot_b(ah, bl) + dot_b(al, bh))


def pack_kernel(dst_ref, tiles_ref, rows_ref, out_ref, stage, sems):
    step = pl.program_id(0)
    steps = pl.num_programs(0)
    slot = lax.rem(step, 2)
    per = tiles_ref.shape[0]

    def copy(at, i, which):
        return pltpu.make_async_copy(
            stage.at[which, i], out_ref.at[dst_ref[at * per + i]], sems.at[which, i])

    @pl.when(step >= 2)
    def _():
        for i in range(per):
            copy(step - 2, i, slot).wait()

    sub = lax.broadcasted_iota(jnp.int32, (TB, TB), 0)
    for i in range(per):
        pick = jnp.where(sub == rows_ref[i:i + 1, :], 1.0, 0.0).astype(BF16)
        tile = tiles_ref[i]
        hi = tile.astype(BF16)
        rest = tile - hi.astype(F32)
        mid = rest.astype(BF16)
        low = (rest - mid.astype(F32)).astype(BF16)
        moved = jnp.dot(pick, hi, preferred_element_type=F32)
        moved = moved + jnp.dot(pick, mid, preferred_element_type=F32)
        moved = moved + jnp.dot(pick, low, preferred_element_type=F32)
        stage[slot, i] = moved
    for i in range(per):
        copy(step, i, slot).start()

    @pl.when(step == steps - 1)
    def _():
        for i in range(per):
            copy(step - 1, i, 1 - slot).wait()
        for i in range(per):
            copy(step, i, slot).wait()


def pack(dst, tiles, rows, slots):
    count = tiles.shape[0]
    per = 8
    return pl.pallas_call(
        pack_kernel,
        grid_spec=pltpu.PrefetchScalarGridSpec(
            num_scalar_prefetch=1,
            grid=(count // per,),
            in_specs=[
                pl.BlockSpec((per, TB, TB), lambda i, d: (i, 0, 0)),
                pl.BlockSpec((per, TB), lambda i, d: (i, 0)),
            ],
            out_specs=pl.BlockSpec(memory_space=pl.ANY),
            scratch_shapes=[
                pltpu.VMEM((2, per, TB, TB), F32),
                pltpu.SemaphoreType.DMA((2, per)),
            ],
        ),
        out_shape=jax.ShapeDtypeStruct((slots, TB, TB), F32),
        name="pack",
    )(dst, tiles, rows)


def bcast_kernel(pa_ref, pc_ref, ga_ref, gc_ref, gr_ref,
                 s1a, s1c, r1a, r1c, loc, ss, rs, fs, fr, xs, xr):
    row = lax.axis_index("row")
    y = lax.axis_index("col")
    core = lax.rem(row, 2)
    z = lax.rem(lax.div(row, 2), 4)
    x = lax.div(row, 8)
    xz = lax.div(row, 2)
    pos = {"x": x, "y": y, "z": z}

    def device(axis, p):
        q = dict(pos)
        q[axis] = p
        return ((q["x"] * 4 + q["z"]) * 2 + core, q["y"])

    def remote(src, dst, send, recv, dev):
        return pltpu.make_async_remote_copy(
            src_ref=src, dst_ref=dst, send_sem=send, recv_sem=recv,
            device_id=dev, device_id_type=MESH)

    def piece_a(q):
        return pa_ref.at[:, q], ga_ref.at[:, y, core, lax.div(q, 4), lax.rem(q, 4)]

    def send_a(q):
        s, d = piece_a(q)
        return remote(s, d, s1a.at[q], r1a.at[0], (q * 2 + core, y))

    to_col = row - 2
    to_core = lax.div(y, 2)

    def piece_c(q):
        return pc_ref.at[q], gc_ref.at[y, lax.div(q, 4), lax.rem(q, 4)]

    def send_c(q):
        s, d = piece_c(q)
        return remote(s, d, s1c.at[q], r1c.at[lax.rem(y, 2)], (q * 2 + to_core, to_col))

    barrier = pltpu.get_barrier_semaphore()

    def greet(dev):
        pl.semaphore_signal(barrier, inc=1, device_id=dev, device_id_type=MESH)

    for axis in "xyz":
        for shift in (1, 3):
            greet(device(axis, lax.rem(pos[axis] + shift, 4)))
    greet((xz * 2 + (1 - core), y))

    is_a = row < 2
    is_c = (row >= 2) & (row < 6)

    def keeps(q):
        return (q == xz) & (to_core == core) & (to_col == y)

    def mine(h):
        return (2 * core + h == y) & (row == y + 2)

    @pl.when(is_a)
    def _():
        @pl.loop(1, 16)
        def _(q):
            greet((q * 2 + core, y))

    @pl.when(jnp.logical_not(is_a))
    def _():
        greet((core, y))

    @pl.when(is_c)
    def _():
        @pl.loop(0, 16)
        def _(q):
            @pl.when(jnp.logical_not(keeps(q)))
            def _():
                greet((q * 2 + to_core, to_col))

    for h in range(2):
        @pl.when(jnp.logical_not(mine(h)))
        def _():
            greet((y + 2, 2 * core + h))

    peers = 7 + jnp.where(is_a, 15, 1)
    peers = peers + jnp.where(is_c, jnp.where((to_core == core) & (to_col == y), 15, 16), 0)
    for h in range(2):
        peers = peers + jnp.where(mine(h), 0, 1)
    pl.semaphore_wait(barrier, peers)

    @pl.when(is_a)
    def _():
        s, d = piece_a(0)
        pltpu.make_async_copy(s, d, loc.at[0]).start()

        @pl.loop(1, 16)
        def _(q):
            send_a(q).start()

    @pl.when(is_c)
    def _():
        @pl.loop(0, 16)
        def _(q):
            @pl.when(keeps(q))
            def _():
                s, d = piece_c(q)
                pltpu.make_async_copy(s, d, loc.at[1]).start()

            @pl.when(jnp.logical_not(keeps(q)))
            def _():
                send_c(q).start()

    chains = []
    for s, order in enumerate((("z", "x", "y"), ("x", "y", "z"), ("y", "z", "x"))):
        chains.append(("a", s, order))
    for s, order in enumerate((("z", "x"), ("x", "z"))):
        chains.append(("c", s, order))
    chains.append(("r", 0, ("y",)))
    total = len(chains)

    def block(kind, s, order, t, p, half=None):
        ind = {}
        for j, a in enumerate(order):
            ind[a] = slice(None) if j < t else (p if j == t else pos[a])
        if kind == "a":
            tail = () if half is None else (pl.ds(8 * half, 8), slice(None))
            fill = () if half is None else tail
            return ga_ref.at[(s, ind["y"], core, ind["x"], ind["z"]) + fill]
        if kind == "r":
            return gr_ref.at[p] if half is None else gr_ref.at[p, pl.ds(8 * half, 8)]
        fill = () if half is None else (pl.ds(24 * half, 24), slice(None))
        return gc_ref.at[(2 * core + s, ind["x"], ind["z"]) + fill]

    sibling = (xz * 2 + (1 - core), y)

    def near(n, t, up):
        kind, s, order = chains[n]
        a = order[t]
        p = pos[a]
        b = block(kind, s, order, t, p)
        src = pc_ref if kind == "r" else b
        return remote(src, b, ss.at[n, t, up], rs.at[n, t, up],
                      device(a, lax.rem(p + (1 if up else 3), 4)))

    def near_wait(n, t, up):
        kind, s, order = chains[n]
        a = order[t]
        b = block(kind, s, order, t, lax.rem(pos[a] + (3 if up else 1), 4))
        remote(b, b, ss.at[n, t, up], rs.at[n, t, up], (row, y)).wait_recv()

    def far(n, t, up):
        kind, s, order = chains[n]
        a = order[t]
        p = pos[a]
        b = block(kind, s, order, t, lax.rem(p + (3 if up else 1), 4), 0 if up else 1)
        return remote(b, b, fs.at[n, t, up], fr.at[n, t, up],
                      device(a, lax.rem(p + (1 if up else 3), 4)))

    def far_wait(n, t, up):
        kind, s, order = chains[n]
        a = order[t]
        b = block(kind, s, order, t, lax.rem(pos[a] + 2, 4), 0 if up else 1)
        remote(b, b, fs.at[n, t, up], fr.at[n, t, up], (row, y)).wait_recv()

    def cross(n, shift):
        kind, s, order = chains[n]
        t = len(order) - 1
        b = block(kind, s, order, t, lax.rem(pos[order[t]] + shift, 4))
        return remote(b, b, xs.at[n, shift], xr.at[n, shift], sibling)

    def cross_wait(n, shift):
        kind, s, order = chains[n]
        t = len(order) - 1
        ind = {}
        for j, a in enumerate(order):
            ind[a] = slice(None) if j < t else lax.rem(pos[a] + shift, 4)
        if kind == "a":
            b = ga_ref.at[s, ind["y"], 1 - core, ind["x"], ind["z"]]
        else:
            b = gc_ref.at[2 * (1 - core) + s, ind["x"], ind["z"]]
        remote(b, b, xs.at[n, shift], xr.at[n, shift], (row, y)).wait_recv()

    diag, column, own = (0, 1, 2), (3, 4), (5,)
    for up in range(2):
        near(5, 0, up).start()
    @pl.when(is_a)
    def _():
        s, d = piece_a(0)
        pltpu.make_async_copy(s, d, loc.at[0]).wait()

    @pl.when(jnp.logical_not(is_a))
    def _():
        s = pa_ref.at[:, 0]
        remote(s, ga_ref.at[:, y, core, x, z], s1a.at[0], r1a.at[0], (row, y)).wait_recv()

    def begin(ns, t):
        for n in ns:
            for up in range(2):
                near(n, t, up).start()

    def forward(ns, t):
        for n in ns:
            for up in range(2):
                near_wait(n, t, up)
                far(n, t, up).start()
                if n < 5 and t == len(chains[n][2]) - 1:
                    cross(n, 3 if up else 1).start()

    def settle(n, t):
        for up in range(2):
            far_wait(n, t, up)

    def advance(ns, t):
        for n in ns:
            settle(n, t)
            begin([n], t + 1)
            if t + 1 == len(chains[n][2]) - 1:
                cross(n, 0).start()

    def finish(ns, t):
        for n in ns:
            settle(n, t)
            cross(n, 2).start()

    begin(diag, 0)
    for h in range(2):
        yy = 2 * core + h

        @pl.when(mine(h))
        def _():
            s, d = piece_c(xz)
            pltpu.make_async_copy(s, d, loc.at[1]).wait()

        @pl.when(jnp.logical_not(mine(h)))
        def _():
            remote(pc_ref.at[0], gc_ref.at[yy, x, z], s1c.at[0], r1c.at[h], (row, y)).wait_recv()

    begin(column, 0)
    forward(diag, 0)
    forward(column, 0)
    advance(diag, 0)
    advance(column, 0)
    forward(diag, 1)
    forward(column, 1)
    advance(diag, 1)
    finish(column, 1)
    forward(own, 0)
    forward(diag, 2)
    finish(diag, 2)
    settle(5, 0)
    for n in range(5):
        for shift in range(4):
            cross_wait(n, shift)
    for n in range(total):
        for t in range(len(chains[n][2])):
            for up in range(2):
                near(n, t, up).wait_send()
                far(n, t, up).wait_send()
    for n in range(5):
        for shift in range(4):
            cross(n, shift).wait_send()

    @pl.when(is_a)
    def _():
        @pl.loop(1, 16)
        def _(q):
            send_a(q).wait_send()

    @pl.when(is_c)
    def _():
        @pl.loop(0, 16)
        def _(q):
            @pl.when(jnp.logical_not(keeps(q)))
            def _():
                send_c(q).wait_send()


def bcast(panel):
    rows, cols = panel.shape
    dma = pltpu.SemaphoreType.DMA
    return pl.pallas_call(
        bcast_kernel,
        in_specs=[pl.BlockSpec(memory_space=pl.ANY)] * 2,
        out_specs=[pl.BlockSpec(memory_space=pl.ANY)] * 3,
        out_shape=[
            jax.ShapeDtypeStruct((3, 4, 2, 4, 4, 16, cols), F32),
            jax.ShapeDtypeStruct((4, 4, 4, 48, cols), F32),
            jax.ShapeDtypeStruct((4, 16, 48, cols), F32),
        ],
        scratch_shapes=[
            dma((16,)), dma((16,)), dma((1,)), dma((2,)), dma((2,)),
            dma((6, 3, 2)), dma((6, 3, 2)), dma((6, 3, 2)), dma((6, 3, 2)),
            dma((5, 4)), dma((5, 4)),
        ],
        compiler_params=pltpu.CompilerParams(has_side_effects=True, collective_id=0),
        name="bcast",
    )(panel.reshape(3, 16, 16, cols), panel.reshape(16, 48, cols))


def wide(v):
    return jnp.broadcast_to(v, (8, 128))


def small_inverse(cols):
    c = [[None] * 8 for _ in range(8)]
    for j in range(8):
        for i in range(j, 8):
            c[i][j] = wide(cols[j][i:i + 1, :])
    t = [[None] * 8 for _ in range(8)]
    for j in range(8):
        r = lax.rsqrt(c[j][j])
        t[j][j] = r
        for i in range(j + 1, 8):
            c[i][j] = c[i][j] * r
        for m in range(j + 1, 8):
            for i in range(m, 8):
                c[i][m] = c[i][m] - c[i][j] * c[m][j]
        for k in range(j):
            s = c[j][k] * t[k][k]
            for m in range(k + 1, j):
                s = s + c[j][m] * t[m][k]
            t[j][k] = -(s * r)
    return t


def factor_block(d):
    row = lax.broadcasted_iota(jnp.int32, (NB, NB), 0)
    col = lax.broadcasted_iota(jnp.int32, (NB, NB), 1)
    eye = jnp.where(row == col, 1.0, 0.0).astype(F32)
    groups = NB // 8
    r = [d[8 * g:8 * g + 8, :] for g in range(groups)]
    w = [eye[8 * g:8 * g + 8, :] for g in range(groups)]
    sub = lax.broadcasted_iota(jnp.int32, (8, NB), 0)
    us, vs = [], []
    for g in range(groups):
        cols = [wide(r[g][:, 8 * g + j:8 * g + j + 1]) for j in range(8)]
        t = small_inverse(cols)
        u = v = None
        for j in range(8):
            part = jnp.zeros((8, NB), F32)
            for i in range(j, 8):
                part = jnp.where(sub == i, t[i][j], part)
            du, dv = part * r[g][j:j + 1, :], part * w[g][j:j + 1, :]
            u, v = (du, dv) if u is None else (u + du, v + dv)
        us.append(u)
        vs.append(v)
        if g + 1 < groups:
            nxt = [wide(r[g + 1][:, 8 * g + j:8 * g + j + 1]) for j in range(8)]
            ra, wa = r[g + 1], w[g + 1]
            for j in range(8):
                m = nxt[0] * t[j][0]
                for k in range(1, j + 1):
                    m = m + nxt[k] * t[j][k]
                ra = ra - m * u[j:j + 1, :]
                wa = wa - m * v[j:j + 1, :]
            r[g + 1], w[g + 1] = ra, wa
        if g + 2 < groups:
            ut = jnp.transpose(u)
            for g2 in range(g + 2, groups):
                blk = ut[8 * g2:8 * g2 + 8, :]
                ra, wa = r[g2], w[g2]
                for j in range(8):
                    m = wide(blk[:, j:j + 1])
                    ra = ra - m * u[j:j + 1, :]
                    wa = wa - m * v[j:j + 1, :]
                r[g2], w[g2] = ra, wa
    upper = jnp.concatenate(us, axis=0)
    inverse = jnp.concatenate(vs, axis=0)
    return jnp.where(col >= row, upper, 0.0), inverse


def chol_kernel(ga_ref, l_ref, w_ref, c_ref):
    def at(i):
        if isinstance(i, int):
            return slice(i * NB, (i + 1) * NB)
        return pl.ds(pl.multiple_of(i * NB, NB), NB)

    def given(i, j):
        r, q = lax.rem(i, 6), lax.rem(i, 2)
        return ga_ref[lax.div(r, 2), lax.div(j, 3), lax.div(i, 6), at(q), at(lax.rem(j, 3))]

    def sym(i, j):
        return 0.5 * (given(i, j) + given(j, i).T)

    l_ref[...] = jnp.zeros_like(l_ref)
    w_ref[...] = jnp.zeros_like(w_ref)
    c_ref[...] = jnp.zeros_like(c_ref)
    d = sym(jnp.int32(0), jnp.int32(0))
    per = 4
    for stage in range(KB // per):
        top = stage * per
        below = slice(top * NB, PW)
        known = slice(0, (top + per) * NB)
        index = top * NB + lax.broadcasted_iota(jnp.int32, (PW - top * NB, NB), 0)

        def step(k, d):
            last = jnp.maximum(k - 1, 0)
            after = jnp.minimum(k + 1, KB - 1)
            column = dot_nt(c_ref[below, :], w_ref[at(last), :])
            fresh = (index >= k * NB) & (k > 0)
            l_ref[below, at(last)] = jnp.where(fresh, column, l_ref[below, at(last)])
            acc = dot_nt(l_ref[below, known], l_ref[at(k), known])
            for i in range(top, KB):
                c_ref[at(i), :] = sym(jnp.int32(i), k) - acc[at(i - top), :]
            row = l_ref[at(after), known]
            rest = sym(after, after) - dot_nt(row, row)

            upper, inverse = factor_block(d)
            w_ref[at(k), :] = inverse
            nxt = dot_nt(c_ref[at(after), :], inverse)
            l_ref[at(after), at(k)] = nxt
            l_ref[at(k), at(k)] = upper.T
            return rest - dot_nt(nxt, nxt)

        d = lax.fori_loop(top, top + per, step, d)


def chol(ga):
    return pl.pallas_call(
        chol_kernel,
        out_shape=[
            jax.ShapeDtypeStruct((PW, PW), F32),
            jax.ShapeDtypeStruct((PW, NB), F32),
        ],
        scratch_shapes=[pltpu.VMEM((PW, NB), F32)],
        compiler_params=pltpu.CompilerParams(vmem_limit_bytes=BIG),
        cost_estimate=pl.CostEstimate(
            flops=60_000_000_000, bytes_accessed=20_000_000, transcendentals=0),
        name="chol",
    )(ga)


def solve_kernel(place_ref, l_ref, w_ref, own_ref, pr_ref, pc_ref, t_ref, f_ref, o_ref,
                 lh, ll, wh, wl, xh, xl, keep):
    row = place_ref[0]
    col = place_ref[1]
    rows = pr_ref.shape[1]
    wide_cols = pr_ref.shape[2]
    nb = 2 * NB

    @pl.loop(0, KB)
    def _(k):
        at = pl.ds(pl.multiple_of(k * NB, NB), NB)
        hi, lo = split2(l_ref[at, :])
        lh[at, :] = hi
        ll[at, :] = lo

    for k in range(KB // 2):
        a, b = 2 * k * NB, (2 * k + 1) * NB
        w1, w2 = w_ref[a:a + NB, :], w_ref[b:b + NB, :]
        cross = l_ref[b:b + NB, a:a + NB]
        mid = jnp.dot(cross, w1, precision=lax.Precision.HIGHEST, preferred_element_type=F32)
        low = -jnp.dot(w2, mid, precision=lax.Precision.HIGHEST, preferred_element_type=F32)
        zero = jnp.zeros((NB, NB), F32)
        hi, lo = split2(jnp.concatenate(
            [jnp.concatenate([w1, zero], axis=1), jnp.concatenate([low, w2], axis=1)], axis=0))
        wh[k] = hi
        wl[k] = lo

    half = rows // 2
    for part, src in enumerate((pr_ref, pc_ref)):
        @pl.loop(0, 2)
        def _(g):
            band = pl.ds(pl.multiple_of(g * half, NB), half)
            for k in range(KB // 2):
                cols = []
                for h in range(2):
                    at = (2 * k + h) * NB
                    j, cut = at // wide_cols, slice(at % wide_cols, at % wide_cols + NB)
                    piece = src[j, band, cut]
                    if part == 0:
                        piece = jnp.where(col == j, own_ref[band, cut], piece)
                    cols.append(piece)
                v = jnp.concatenate(cols, axis=1)
                here = slice(k * nb, (k + 1) * nb)
                if k > 0:
                    done = slice(0, k * nb)
                    v = v - dot3(xh[part, band, done], xl[part, band, done],
                                 lh[here, done], ll[here, done])
                vh, vl = split2(v)
                v = dot3(vh, vl, wh[k], wl[k])
                hi, lo = split2(v)
                xh[part, band, here] = hi
                xl[part, band, here] = lo
                if part == 0:
                    for h in range(2):
                        at = (2 * k + h) * NB
                        keep[at // wide_cols, band, at % wide_cols:at % wide_cols + NB] = (
                            v[:, h * NB:(h + 1) * NB])

    @pl.when(row >= 2)
    def _():
        f_ref[...] = keep[col]

        @pl.loop(0, rows // 256)
        def _(i):
            at = pl.ds(pl.multiple_of(i * 256, 256), 256)
            o_ref[at, :] = t_ref[at, :] - dot3(xh[0, at, :], xl[0, at, :], xh[1], xl[1])

    @pl.when(row < 2)
    def _():
        first = pl.ds(pl.multiple_of(row * rows, NB), rows)
        f_ref[...] = l_ref[first, pl.ds(pl.multiple_of(col * wide_cols, NB), wide_cols)]
        o_ref[...] = t_ref[...]


def solve(place, factor, inverse, own, mine, theirs, trailing):
    n, rows, cols = mine.shape
    smem = pl.BlockSpec(memory_space=pltpu.SMEM)
    vmem = pl.BlockSpec(memory_space=pltpu.VMEM)
    return pl.pallas_call(
        solve_kernel,
        in_specs=[smem] + [vmem] * 6,
        out_specs=[vmem, vmem],
        out_shape=[
            jax.ShapeDtypeStruct((rows, cols), F32),
            jax.ShapeDtypeStruct(trailing.shape, F32),
        ],
        scratch_shapes=[
            pltpu.VMEM((PW, PW), BF16), pltpu.VMEM((PW, PW), BF16),
            pltpu.VMEM((KB // 2, 2 * NB, 2 * NB), BF16), pltpu.VMEM((KB // 2, 2 * NB, 2 * NB), BF16),
            pltpu.VMEM((2, rows, PW), BF16), pltpu.VMEM((2, rows, PW), BF16),
            pltpu.VMEM((n, rows, cols), F32),
        ],
        compiler_params=pltpu.CompilerParams(vmem_limit_bytes=BIG),
        cost_estimate=pl.CostEstimate(
            flops=30_000_000_000, bytes_accessed=30_000_000, transcendentals=0),
        name="solve",
    )(place, factor, inverse, own, mine, theirs, trailing)


def add_kernel(target_ref, tiles_ref, base_ref, out_ref):
    step = pl.program_id(0)
    per = tiles_ref.shape[0]
    tile_cols = out_ref.shape[1] // TB

    @pl.when(step == 0)
    def _():
        out_ref[...] = base_ref[...]

    for i in range(per):
        target = target_ref[step * per + i]

        @pl.when(target >= 0)
        def _():
            r = pl.ds(pl.multiple_of(lax.div(target, tile_cols) * TB, TB), TB)
            c = pl.ds(pl.multiple_of(lax.rem(target, tile_cols) * TB, TB), TB)
            out_ref[r, c] = out_ref[r, c] + tiles_ref[i]


def extend_add(target, tiles, base):
    per = 16
    return pl.pallas_call(
        add_kernel,
        grid_spec=pltpu.PrefetchScalarGridSpec(
            num_scalar_prefetch=1,
            grid=(tiles.shape[0] // per,),
            in_specs=[
                pl.BlockSpec((per, TB, TB), lambda i, t: (i, 0, 0)),
                pl.BlockSpec(base.shape, lambda i, t: (0, 0)),
            ],
            out_specs=pl.BlockSpec(base.shape, lambda i, t: (0, 0)),
        ),
        out_shape=jax.ShapeDtypeStruct(base.shape, F32),
        compiler_params=pltpu.CompilerParams(vmem_limit_bytes=32 << 20),
        name="extend_add",
    )(target, tiles, base)


def body(panel, trailing, child_tiles, child_owner, child_tile, child_rows):
    devices = lax.axis_size("row") * lax.axis_size("col")
    count = child_owner.shape[0]
    cap = 2
    both = ("row", "col")
    order = jnp.arange(count, dtype=jnp.int32)
    same = child_owner[:, None] == child_owner[None, :]
    rank = jnp.sum(jnp.where(same & (order[None, :] < order[:, None]), 1, 0), axis=1)
    dst = (child_owner * cap + rank).astype(jnp.int32)
    slots = devices * cap
    hit = dst[:, None] == jnp.arange(slots, dtype=jnp.int32)[None, :]
    target = (jnp.sum(jnp.where(hit, child_tile[:, None] + 1, 0), axis=0) - 1).astype(jnp.int32)
    got_target = lax.all_to_all(
        target.reshape(devices, cap), both, split_axis=0, concat_axis=0, tiled=True)
    packed = pack(dst, child_tiles, child_rows, slots)
    ga, gc, mine = bcast(panel)
    packed, ga = lax.optimization_barrier((packed, ga))
    got = lax.all_to_all(
        packed.reshape(devices, cap, TB, TB), both, split_axis=0, concat_axis=0, tiled=True)
    row_index, col_index = lax.axis_index("row"), lax.axis_index("col")
    factor, inverse = chol(ga.reshape(3, 4, 2, 256, panel.shape[1]))
    place = jnp.stack([row_index, col_index]).astype(jnp.int32)
    factor_panel, base = solve(
        place, factor, inverse, panel, mine.reshape(4, *panel.shape), gc.reshape(4, *panel.shape), trailing)
    new_trailing = extend_add(got_target.reshape(-1), got.reshape(-1, TB, TB), base)
    return factor_panel, new_trailing


def solution(mesh):
    in_specs = (
        P("row", "col"),
        P("row", "col"),
        P(("row", "col"), None, None),
        P(("row", "col")),
        P(("row", "col")),
        P(("row", "col"), None),
    )
    out_specs = (P("row", "col"), P("row", "col"))
    return jax.shard_map(body, mesh=mesh, in_specs=in_specs, out_specs=out_specs, check_vma=False)
```

```python
import functools

import jax
import jax.numpy as jnp
from jax import lax
from jax.experimental import pallas as pl
from jax.experimental.pallas import tpu as pltpu
from jax.sharding import PartitionSpec as P

PW = 1536
NB = 128
KB = PW // NB
TB = 128
MESH = pl.DeviceIdType.MESH
F32 = jnp.float32
BF16 = jnp.bfloat16
BIG = 60 << 20
PER = 32
ORDERS = (("z", "x", "y"), ("x", "y", "z"), ("y", "z", "x"))


def dot_nt(a, b):
    return lax.dot_general(
        a, b, (((1,), (1,)), ((), ())),
        precision=lax.Precision.HIGHEST, preferred_element_type=F32)


def dot_b(a, b):
    return lax.dot_general(a, b, (((1,), (1,)), ((), ())), preferred_element_type=F32)


def split2(v):
    hi = v.astype(BF16)
    return hi, (v - hi.astype(F32)).astype(BF16)


def dot3(ah, al, bh, bl):
    return dot_b(ah, bh) + (dot_b(ah, bl) + dot_b(al, bh))


def pack_kernel(dst_ref, tiles_ref, rows_ref, out_ref, stage, sems):
    step = pl.program_id(0)
    steps = pl.num_programs(0)
    slot = lax.rem(step, 2)
    per = tiles_ref.shape[0]

    def copy(at, i, which):
        return pltpu.make_async_copy(
            stage.at[which, i], out_ref.at[dst_ref[at * per + i]], sems.at[which, i])

    @pl.when(step >= 2)
    def _():
        for i in range(per):
            copy(step - 2, i, slot).wait()

    sub = lax.broadcasted_iota(jnp.int32, (TB, TB), 0)
    for i in range(per):
        pick = jnp.where(sub == rows_ref[i:i + 1, :], 1.0, 0.0).astype(BF16)
        tile = tiles_ref[i]
        hi = tile.astype(BF16)
        rest = tile - hi.astype(F32)
        mid = rest.astype(BF16)
        low = (rest - mid.astype(F32)).astype(BF16)
        moved = jnp.dot(pick, hi, preferred_element_type=F32)
        moved = moved + jnp.dot(pick, mid, preferred_element_type=F32)
        moved = moved + jnp.dot(pick, low, preferred_element_type=F32)
        stage[slot, i] = moved
    for i in range(per):
        copy(step, i, slot).start()

    @pl.when(step == steps - 1)
    def _():
        for i in range(per):
            copy(step - 1, i, 1 - slot).wait()
        for i in range(per):
            copy(step, i, slot).wait()


def pack(dst, tiles, rows, slots):
    count = tiles.shape[0]
    per = PER
    return pl.pallas_call(
        pack_kernel,
        grid_spec=pltpu.PrefetchScalarGridSpec(
            num_scalar_prefetch=1,
            grid=(count // per,),
            in_specs=[
                pl.BlockSpec((per, TB, TB), lambda i, d: (i, 0, 0)),
                pl.BlockSpec((per, TB), lambda i, d: (i, 0)),
            ],
            out_specs=pl.BlockSpec(memory_space=pl.ANY),
            scratch_shapes=[
                pltpu.VMEM((2, per, TB, TB), F32),
                pltpu.SemaphoreType.DMA((2, per)),
            ],
        ),
        out_shape=jax.ShapeDtypeStruct((slots, TB, TB), F32),
        name="pack",
    )(dst, tiles, rows)


def bcast_kernel(pa_ref, pc_ref, pt_ref, ga_ref, gc_ref, gr_ref, gt_ref,
                 s1a, s1c, r1a, r1c, loc, ss, rs, fs, fr, xs, xr):
    row = lax.axis_index("row")
    y = lax.axis_index("col")
    core = lax.rem(row, 2)
    z = lax.rem(lax.div(row, 2), 4)
    x = lax.div(row, 8)
    xz = lax.div(row, 2)
    pos = {"x": x, "y": y, "z": z}

    def device(axis, p):
        q = dict(pos)
        q[axis] = p
        return ((q["x"] * 4 + q["z"]) * 2 + core, q["y"])

    def remote(src, dst, send, recv, dev):
        return pltpu.make_async_remote_copy(
            src_ref=src, dst_ref=dst, send_sem=send, recv_sem=recv,
            device_id=dev, device_id_type=MESH)

    def piece_a(q):
        return pa_ref.at[:, q], ga_ref.at[:, y, core, lax.div(q, 4), lax.rem(q, 4)]

    def send_a(q):
        s, d = piece_a(q)
        return remote(s, d, s1a.at[q], r1a.at[0], (q * 2 + core, y))

    to_col = row - 2
    to_core = lax.div(y, 2)

    def piece_c(q):
        return pc_ref.at[q], gc_ref.at[y, lax.div(q, 4), lax.rem(q, 4)]

    def send_c(q):
        s, d = piece_c(q)
        return remote(s, d, s1c.at[q], r1c.at[lax.rem(y, 2)], (q * 2 + to_core, to_col))

    barrier = pltpu.get_barrier_semaphore()

    def greet(dev):
        pl.semaphore_signal(barrier, inc=1, device_id=dev, device_id_type=MESH)

    for axis in "xyz":
        for shift in (1, 3):
            greet(device(axis, lax.rem(pos[axis] + shift, 4)))
    greet((xz * 2 + (1 - core), y))

    is_a = row < 2
    is_c = (row >= 2) & (row < 6)

    def keeps(q):
        return (q == xz) & (to_core == core) & (to_col == y)

    def mine(h):
        return (2 * core + h == y) & (row == y + 2)

    @pl.when(is_a)
    def _():
        @pl.loop(1, 16)
        def _(q):
            greet((q * 2 + core, y))

    @pl.when(jnp.logical_not(is_a))
    def _():
        greet((core, y))

    @pl.when(is_c)
    def _():
        @pl.loop(0, 16)
        def _(q):
            @pl.when(jnp.logical_not(keeps(q)))
            def _():
                greet((q * 2 + to_core, to_col))

    for h in range(2):
        @pl.when(jnp.logical_not(mine(h)))
        def _():
            greet((y + 2, 2 * core + h))

    peers = 7 + jnp.where(is_a, 15, 1)
    peers = peers + jnp.where(is_c, jnp.where((to_core == core) & (to_col == y), 15, 16), 0)
    for h in range(2):
        peers = peers + jnp.where(mine(h), 0, 1)
    pl.semaphore_wait(barrier, peers)

    @pl.when(is_a)
    def _():
        s, d = piece_a(0)
        pltpu.make_async_copy(s, d, loc.at[0]).start()

        @pl.loop(1, 16)
        def _(q):
            send_a(q).start()

    @pl.when(is_c)
    def _():
        @pl.loop(0, 16)
        def _(q):
            @pl.when(keeps(q))
            def _():
                s, d = piece_c(q)
                pltpu.make_async_copy(s, d, loc.at[1]).start()

            @pl.when(jnp.logical_not(keeps(q)))
            def _():
                send_c(q).start()

    chains = []
    for s, order in enumerate(ORDERS):
        chains.append(("a", s, order))
    for s, order in enumerate((("z", "x"), ("x", "z"))):
        chains.append(("c", s, order))
    chains.append(("r", 0, ("y",)))
    chains.append(("t", 0, ("z", "x", "y")))
    shared = [n for n in range(len(chains)) if chains[n][0] != "r"]
    total = len(chains)

    def block(kind, s, order, t, p, half=None, cut=None):
        ind = {}
        for j, a in enumerate(order):
            ind[a] = slice(None) if j < t else (p if j == t else pos[a])
        if cut is not None and kind != "r":
            ind[order[0]] = cut
        if kind == "a":
            tail = () if half is None else (pl.ds(8 * half, 8), slice(None))
            fill = () if half is None else tail
            return ga_ref.at[(s, ind["y"], core, ind["x"], ind["z"]) + fill]
        if kind == "r":
            first, size = (0, 16) if half is None else (8 * half, 8)
            if cut is not None:
                size = size // 4
                first = first + cut * size
            return gr_ref.at[p, pl.ds(first, size)]
        if kind == "t":
            fill = () if half is None else (pl.ds(8 * half, 8), slice(None))
            return gt_ref.at[(ind["y"], core, ind["x"], ind["z"]) + fill]
        fill = () if half is None else (pl.ds(24 * half, 24), slice(None))
        return gc_ref.at[(2 * core + s, ind["x"], ind["z"]) + fill]

    sibling = (xz * 2 + (1 - core), y)

    def cuts(n, t):
        if chains[n][0] == "t":
            return (None,)
        return range(4) if t > 0 or chains[n][0] == "r" else (None,)

    def near(n, t, up, cut=None):
        kind, s, order = chains[n]
        a = order[t]
        p = pos[a]
        b = block(kind, s, order, t, p, None, cut)
        src = b
        if kind == "r":
            src = pc_ref if cut is None else pc_ref.at[pl.ds(cut * 4, 4)]
        return remote(src, b, ss.at[n, t, up], rs.at[n, t, up],
                      device(a, lax.rem(p + (1 if up else 3), 4)))

    def near_wait(n, t, up):
        kind, s, order = chains[n]
        a = order[t]
        b = block(kind, s, order, t, lax.rem(pos[a] + (3 if up else 1), 4))
        remote(b, b, ss.at[n, t, up], rs.at[n, t, up], (row, y)).wait_recv()

    def far(n, t, up, cut=None):
        kind, s, order = chains[n]
        a = order[t]
        p = pos[a]
        b = block(kind, s, order, t, lax.rem(p + (3 if up else 1), 4), 0 if up else 1, cut)
        return remote(b, b, fs.at[n, t, up], fr.at[n, t, up],
                      device(a, lax.rem(p + (1 if up else 3), 4)))

    def far_wait(n, t, up):
        kind, s, order = chains[n]
        a = order[t]
        b = block(kind, s, order, t, lax.rem(pos[a] + 2, 4), 0 if up else 1)
        remote(b, b, fs.at[n, t, up], fr.at[n, t, up], (row, y)).wait_recv()

    def cross(n, shift, cut=None):
        kind, s, order = chains[n]
        t = len(order) - 1
        b = block(kind, s, order, t, lax.rem(pos[order[t]] + shift, 4), None, cut)
        return remote(b, b, xs.at[n, shift], xr.at[n, shift], sibling)

    def cross_wait(n, shift):
        kind, s, order = chains[n]
        t = len(order) - 1
        ind = {}
        for j, a in enumerate(order):
            ind[a] = slice(None) if j < t else lax.rem(pos[a] + shift, 4)
        if kind == "a":
            b = ga_ref.at[s, ind["y"], 1 - core, ind["x"], ind["z"]]
        elif kind == "t":
            b = gt_ref.at[ind["y"], 1 - core, ind["x"], ind["z"]]
        else:
            b = gc_ref.at[2 * (1 - core) + s, ind["x"], ind["z"]]
        remote(b, b, xs.at[n, shift], xr.at[n, shift], (row, y)).wait_recv()

    diag, column, own = (6, 0, 1, 2), (3, 4), (5,)
    table = pltpu.make_async_copy(pt_ref, gt_ref.at[y, core, x, z], loc.at[2])
    table.start()
    for up in range(2):
        for cut in cuts(5, 0):
            near(5, 0, up, cut).start()
    @pl.when(is_a)
    def _():
        s, d = piece_a(0)
        pltpu.make_async_copy(s, d, loc.at[0]).wait()

    @pl.when(jnp.logical_not(is_a))
    def _():
        s = pa_ref.at[:, 0]
        remote(s, ga_ref.at[:, y, core, x, z], s1a.at[0], r1a.at[0], (row, y)).wait_recv()

    def share(n, shift):
        for cut in (None,) if chains[n][0] == "t" else range(4):
            cross(n, shift, cut).start()

    def begin(ns, t):
        for n in ns:
            for up in range(2):
                for cut in cuts(n, t):
                    near(n, t, up, cut).start()

    def forward(ns, t):
        for n in ns:
            for up in range(2):
                near_wait(n, t, up)
                for cut in cuts(n, t):
                    far(n, t, up, cut).start()
                if n in shared and t == len(chains[n][2]) - 1:
                    share(n, 3 if up else 1)

    def settle(n, t):
        for up in range(2):
            far_wait(n, t, up)

    def advance(ns, t):
        for n in ns:
            settle(n, t)
            begin([n], t + 1)
            if t + 1 == len(chains[n][2]) - 1:
                share(n, 0)

    def finish(ns, t):
        for n in ns:
            settle(n, t)
            share(n, 2)

    table.wait()
    begin(diag, 0)
    for h in range(2):
        yy = 2 * core + h

        @pl.when(mine(h))
        def _():
            s, d = piece_c(xz)
            pltpu.make_async_copy(s, d, loc.at[1]).wait()

        @pl.when(jnp.logical_not(mine(h)))
        def _():
            remote(pc_ref.at[0], gc_ref.at[yy, x, z], s1c.at[0], r1c.at[h], (row, y)).wait_recv()

    begin(column, 0)
    forward(diag, 0)
    forward(column, 0)
    advance(diag, 0)
    advance(column, 0)
    forward(diag, 1)
    forward(column, 1)
    advance(diag, 1)
    finish(column, 1)
    forward(own, 0)
    forward(diag, 2)
    finish(diag, 2)
    settle(5, 0)
    for n in shared:
        for shift in range(4):
            cross_wait(n, shift)
    for n in range(total):
        for t in range(len(chains[n][2])):
            for up in range(2):
                near(n, t, up).wait_send()
                far(n, t, up).wait_send()
    for n in shared:
        for shift in range(4):
            cross(n, shift).wait_send()

    @pl.when(is_a)
    def _():
        @pl.loop(1, 16)
        def _(q):
            send_a(q).wait_send()

    @pl.when(is_c)
    def _():
        @pl.loop(0, 16)
        def _(q):
            @pl.when(jnp.logical_not(keeps(q)))
            def _():
                send_c(q).wait_send()


def bcast(panel, table):
    rows, cols = panel.shape
    dma = pltpu.SemaphoreType.DMA
    return pl.pallas_call(
        bcast_kernel,
        in_specs=[pl.BlockSpec(memory_space=pl.ANY)] * 3,
        out_specs=[pl.BlockSpec(memory_space=pl.ANY)] * 4,
        out_shape=[
            jax.ShapeDtypeStruct((3, 4, 2, 4, 4, 16, cols), F32),
            jax.ShapeDtypeStruct((4, 4, 4, 48, cols), F32),
            jax.ShapeDtypeStruct((4, 16, 48, cols), F32),
            jax.ShapeDtypeStruct((4, 2, 4, 4) + table.shape, F32),
        ],
        scratch_shapes=[
            dma((16,)), dma((16,)), dma((1,)), dma((2,)), dma((3,)),
            dma((7, 3, 2)), dma((7, 3, 2)), dma((7, 3, 2)), dma((7, 3, 2)),
            dma((7, 4)), dma((7, 4)),
        ],
        compiler_params=pltpu.CompilerParams(has_side_effects=True, collective_id=0),
        name="bcast",
    )(panel.reshape(3, 16, 16, cols), panel.reshape(16, 48, cols), table)


def wide(v):
    return jnp.broadcast_to(v, (8, 128))


def small_inverse(cols):
    c = [[None] * 8 for _ in range(8)]
    for j in range(8):
        for i in range(j, 8):
            c[i][j] = wide(cols[j][i:i + 1, :])
    t = [[None] * 8 for _ in range(8)]
    for j in range(8):
        r = lax.rsqrt(c[j][j])
        t[j][j] = r
        for i in range(j + 1, 8):
            c[i][j] = c[i][j] * r
        for m in range(j + 1, 8):
            for i in range(m, 8):
                c[i][m] = c[i][m] - c[i][j] * c[m][j]
        for k in range(j):
            s = c[j][k] * t[k][k]
            for m in range(k + 1, j):
                s = s + c[j][m] * t[m][k]
            t[j][k] = -(s * r)
    return t


def factor_block(d):
    row = lax.broadcasted_iota(jnp.int32, (NB, NB), 0)
    col = lax.broadcasted_iota(jnp.int32, (NB, NB), 1)
    eye = jnp.where(row == col, 1.0, 0.0).astype(F32)
    groups = NB // 8
    r = [d[8 * g:8 * g + 8, :] for g in range(groups)]
    w = [eye[8 * g:8 * g + 8, :] for g in range(groups)]
    sub = lax.broadcasted_iota(jnp.int32, (8, NB), 0)
    us, vs = [], []
    for g in range(groups):
        cols = [wide(r[g][:, 8 * g + j:8 * g + j + 1]) for j in range(8)]
        t = small_inverse(cols)
        u = v = None
        for j in range(8):
            part = jnp.zeros((8, NB), F32)
            for i in range(j, 8):
                part = jnp.where(sub == i, t[i][j], part)
            du, dv = part * r[g][j:j + 1, :], part * w[g][j:j + 1, :]
            u, v = (du, dv) if u is None else (u + du, v + dv)
        us.append(u)
        vs.append(v)
        if g + 1 < groups:
            nxt = [wide(r[g + 1][:, 8 * g + j:8 * g + j + 1]) for j in range(8)]
            ra, wa = r[g + 1], w[g + 1]
            for j in range(8):
                m = nxt[0] * t[j][0]
                for k in range(1, j + 1):
                    m = m + nxt[k] * t[j][k]
                ra = ra - m * u[j:j + 1, :]
                wa = wa - m * v[j:j + 1, :]
            r[g + 1], w[g + 1] = ra, wa
        if g + 2 < groups:
            ut = jnp.transpose(u)
            for g2 in range(g + 2, groups):
                blk = ut[8 * g2:8 * g2 + 8, :]
                ra, wa = r[g2], w[g2]
                for j in range(8):
                    m = wide(blk[:, j:j + 1])
                    ra = ra - m * u[j:j + 1, :]
                    wa = wa - m * v[j:j + 1, :]
                r[g2], w[g2] = ra, wa
    upper = jnp.concatenate(us, axis=0)
    inverse = jnp.concatenate(vs, axis=0)
    return jnp.where(col >= row, upper, 0.0), inverse


def chol_kernel(ga_ref, l_ref, w_ref, c_ref):
    def at(i):
        if isinstance(i, int):
            return slice(i * NB, (i + 1) * NB)
        return pl.ds(pl.multiple_of(i * NB, NB), NB)

    def given(i, j):
        r, q = lax.rem(i, 6), lax.rem(i, 2)
        return ga_ref[lax.div(r, 2), lax.div(j, 3), lax.div(i, 6), at(q), at(lax.rem(j, 3))]

    def sym(i, j):
        return 0.5 * (given(i, j) + given(j, i).T)

    l_ref[...] = jnp.zeros_like(l_ref)
    w_ref[...] = jnp.zeros_like(w_ref)
    c_ref[...] = jnp.zeros_like(c_ref)
    d = sym(jnp.int32(0), jnp.int32(0))
    per = 4
    for stage in range(KB // per):
        top = stage * per
        below = slice(top * NB, PW)
        known = slice(0, (top + per) * NB)
        index = top * NB + lax.broadcasted_iota(jnp.int32, (PW - top * NB, NB), 0)

        def step(k, d):
            last = jnp.maximum(k - 1, 0)
            after = jnp.minimum(k + 1, KB - 1)
            column = dot_nt(c_ref[below, :], w_ref[at(last), :])
            fresh = (index >= k * NB) & (k > 0)
            l_ref[below, at(last)] = jnp.where(fresh, column, l_ref[below, at(last)])
            acc = dot_nt(l_ref[below, known], l_ref[at(k), known])
            for i in range(top, KB):
                c_ref[at(i), :] = sym(jnp.int32(i), k) - acc[at(i - top), :]
            row = l_ref[at(after), known]
            rest = sym(after, after) - dot_nt(row, row)

            upper, inverse = factor_block(d)
            w_ref[at(k), :] = inverse
            nxt = dot_nt(c_ref[at(after), :], inverse)
            l_ref[at(after), at(k)] = nxt
            l_ref[at(k), at(k)] = upper.T
            return rest - dot_nt(nxt, nxt)

        d = lax.fori_loop(top, top + per, step, d)


def chol(ga):
    return pl.pallas_call(
        chol_kernel,
        out_shape=[
            jax.ShapeDtypeStruct((PW, PW), F32),
            jax.ShapeDtypeStruct((PW, NB), F32),
        ],
        scratch_shapes=[pltpu.VMEM((PW, NB), F32)],
        compiler_params=pltpu.CompilerParams(vmem_limit_bytes=BIG),
        cost_estimate=pl.CostEstimate(
            flops=60_000_000_000, bytes_accessed=20_000_000, transcendentals=0),
        name="chol",
    )(ga)


def solve_kernel(place_ref, l_ref, w_ref, own_ref, pr_ref, pc_ref, t_ref, f_ref, o_ref,
                 lh, ll, wh, wl, xh, xl, keep):
    row = place_ref[0]
    col = place_ref[1]
    rows = pr_ref.shape[1]
    wide_cols = pr_ref.shape[2]
    nb = 2 * NB

    @pl.loop(0, KB)
    def _(k):
        at = pl.ds(pl.multiple_of(k * NB, NB), NB)
        hi, lo = split2(l_ref[at, :])
        lh[at, :] = hi
        ll[at, :] = lo

    for k in range(KB // 2):
        a, b = 2 * k * NB, (2 * k + 1) * NB
        w1, w2 = w_ref[a:a + NB, :], w_ref[b:b + NB, :]
        cross = l_ref[b:b + NB, a:a + NB]
        mid = jnp.dot(cross, w1, precision=lax.Precision.HIGHEST, preferred_element_type=F32)
        low = -jnp.dot(w2, mid, precision=lax.Precision.HIGHEST, preferred_element_type=F32)
        zero = jnp.zeros((NB, NB), F32)
        hi, lo = split2(jnp.concatenate(
            [jnp.concatenate([w1, zero], axis=1), jnp.concatenate([low, w2], axis=1)], axis=0))
        wh[k] = hi
        wl[k] = lo

    half = rows // 2
    for part, src in enumerate((pr_ref, pc_ref)):
        @pl.loop(0, 2)
        def _(g):
            band = pl.ds(pl.multiple_of(g * half, NB), half)
            for k in range(KB // 2):
                cols = []
                for h in range(2):
                    at = (2 * k + h) * NB
                    j, cut = at // wide_cols, slice(at % wide_cols, at % wide_cols + NB)
                    piece = src[j, band, cut]
                    if part == 0:
                        piece = jnp.where(col == j, own_ref[band, cut], piece)
                    cols.append(piece)
                v = jnp.concatenate(cols, axis=1)
                here = slice(k * nb, (k + 1) * nb)
                if k > 0:
                    done = slice(0, k * nb)
                    v = v - dot3(xh[part, band, done], xl[part, band, done],
                                 lh[here, done], ll[here, done])
                vh, vl = split2(v)
                v = dot3(vh, vl, wh[k], wl[k])
                hi, lo = split2(v)
                xh[part, band, here] = hi
                xl[part, band, here] = lo
                if part == 0:
                    for h in range(2):
                        at = (2 * k + h) * NB
                        keep[at // wide_cols, band, at % wide_cols:at % wide_cols + NB] = (
                            v[:, h * NB:(h + 1) * NB])

    @pl.when(row >= 2)
    def _():
        f_ref[...] = keep[col]

        @pl.loop(0, rows // 256)
        def _(i):
            at = pl.ds(pl.multiple_of(i * 256, 256), 256)
            o_ref[at, :] = t_ref[at, :] - dot3(xh[0, at, :], xl[0, at, :], xh[1], xl[1])

    @pl.when(row < 2)
    def _():
        first = pl.ds(pl.multiple_of(row * rows, NB), rows)
        f_ref[...] = l_ref[first, pl.ds(pl.multiple_of(col * wide_cols, NB), wide_cols)]
        o_ref[...] = t_ref[...]


def solve(place, factor, inverse, own, mine, theirs, trailing):
    n, rows, cols = mine.shape
    smem = pl.BlockSpec(memory_space=pltpu.SMEM)
    vmem = pl.BlockSpec(memory_space=pltpu.VMEM)
    return pl.pallas_call(
        solve_kernel,
        in_specs=[smem] + [vmem] * 6,
        out_specs=[vmem, vmem],
        out_shape=[
            jax.ShapeDtypeStruct((rows, cols), F32),
            jax.ShapeDtypeStruct(trailing.shape, F32),
        ],
        scratch_shapes=[
            pltpu.VMEM((PW, PW), BF16), pltpu.VMEM((PW, PW), BF16),
            pltpu.VMEM((KB // 2, 2 * NB, 2 * NB), BF16), pltpu.VMEM((KB // 2, 2 * NB, 2 * NB), BF16),
            pltpu.VMEM((2, rows, PW), BF16), pltpu.VMEM((2, rows, PW), BF16),
            pltpu.VMEM((n, rows, cols), F32),
        ],
        compiler_params=pltpu.CompilerParams(vmem_limit_bytes=BIG),
        cost_estimate=pl.CostEstimate(
            flops=30_000_000_000, bytes_accessed=30_000_000, transcendentals=0),
        name="solve",
    )(place, factor, inverse, own, mine, theirs, trailing)


def add_kernel(target_ref, *refs):
    *tile_refs, base_ref, out_ref, total = refs
    step = pl.program_id(0)
    streams = len(tile_refs)
    per = streams * tile_refs[0].shape[0]
    rows = out_ref.shape[0]
    tile_cols = out_ref.shape[1] // TB

    @pl.when(step == 0)
    def _():
        total[0:rows, :] = base_ref[...]

    spare = (rows // TB) * tile_cols
    for i in range(per):
        sizes = per // streams
        at = (i % streams) * (pl.num_programs(0) * sizes) + step * sizes + i // streams
        target = target_ref[at]
        target = jnp.where(target < 0, spare, target)
        r = pl.ds(pl.multiple_of(lax.div(target, tile_cols) * TB, TB), TB)
        c = pl.ds(pl.multiple_of(lax.rem(target, tile_cols) * TB, TB), TB)
        total[r, c] = total[r, c] + tile_refs[i % streams][i // streams]

    @pl.when(step == pl.num_programs(0) - 1)
    def _():
        out_ref[...] = total[0:rows, :]


def stream_block(first, i, t):
    return (first + i, 0, 0)


def extend_add(target, tiles, base):
    streams, size = 4, 8
    steps = tiles.shape[0] // (streams * size)
    return pl.pallas_call(
        add_kernel,
        grid_spec=pltpu.PrefetchScalarGridSpec(
            num_scalar_prefetch=1,
            grid=(steps,),
            in_specs=[
                pl.BlockSpec((size, TB, TB), functools.partial(stream_block, s * steps))
                for s in range(streams)
            ] + [
                pl.BlockSpec(base.shape, lambda i, t: (0, 0)),
            ],
            out_specs=pl.BlockSpec(base.shape, lambda i, t: (0, 0)),
            scratch_shapes=[pltpu.VMEM((base.shape[0] + TB, base.shape[1]), F32)],
        ),
        out_shape=jax.ShapeDtypeStruct(base.shape, F32),
        compiler_params=pltpu.CompilerParams(vmem_limit_bytes=40 << 20),
        name="extend_add",
    )(target, *([tiles] * streams), base)


def body(panel, trailing, child_tiles, child_owner, child_tile, child_rows):
    devices = lax.axis_size("row") * lax.axis_size("col")
    count = child_owner.shape[0]
    cap = 2
    both = ("row", "col")
    order = jnp.arange(count, dtype=jnp.int32)
    same = child_owner[:, None] == child_owner[None, :]
    rank = jnp.sum(jnp.where(same & (order[None, :] < order[:, None]), 1, 0), axis=1)
    dst = (child_owner * cap + rank).astype(jnp.int32)
    slots = devices * cap
    hit = dst[:, None] == jnp.arange(slots, dtype=jnp.int32)[None, :]
    target = (jnp.sum(jnp.where(hit, child_tile[:, None] + 1, 0), axis=0) - 1).astype(jnp.int32)
    table = jnp.pad(target.reshape(devices, cap).T.astype(F32), ((0, 14), (0, 0)))
    packed = pack(dst, child_tiles, child_rows, slots)
    ga, gc, mine, tables = bcast(panel, table)
    packed, ga = lax.optimization_barrier((packed, ga))
    got = lax.all_to_all(
        packed.reshape(devices, cap, TB, TB), both, split_axis=0, concat_axis=0, tiled=True)
    row_index, col_index = lax.axis_index("row"), lax.axis_index("col")
    me = row_index * lax.axis_size("col") + col_index
    lane = jnp.arange(devices, dtype=jnp.int32)
    picked = jnp.sum(jnp.where(lane == me, tables[..., :cap, :], 0.0), axis=-1)
    got_target = picked.transpose(2, 3, 1, 0, 4).astype(jnp.int32)
    factor, inverse = chol(ga.reshape(3, 4, 2, 256, panel.shape[1]))
    place = jnp.stack([row_index, col_index]).astype(jnp.int32)
    factor_panel, base = solve(
        place, factor, inverse, panel, mine.reshape(4, *panel.shape), gc.reshape(4, *panel.shape), trailing)
    new_trailing = extend_add(got_target.reshape(-1), got.reshape(-1, TB, TB), base)
    return factor_panel, new_trailing


def solution(mesh):
    in_specs = (
        P("row", "col"),
        P("row", "col"),
        P(("row", "col"), None, None),
        P(("row", "col")),
        P(("row", "col")),
        P(("row", "col"), None),
    )
    out_specs = (P("row", "col"), P("row", "col"))
    return jax.shard_map(body, mesh=mesh, in_specs=in_specs, out_specs=out_specs, check_vma=False)
```

```python
import functools

import jax
import jax.numpy as jnp
from jax import lax
from jax.experimental import pallas as pl
from jax.experimental.pallas import tpu as pltpu
from jax.sharding import PartitionSpec as P

PW = 1536
NB = 128
KB = PW // NB
TB = 128
MESH = pl.DeviceIdType.MESH
F32 = jnp.float32
BF16 = jnp.bfloat16
BIG = 60 << 20
PER = 32
ORDERS = (("z", "x", "y"), ("x", "y", "z"), ("y", "z", "x"))


def dot_nt(a, b):
    return lax.dot_general(
        a, b, (((1,), (1,)), ((), ())),
        precision=lax.Precision.HIGHEST, preferred_element_type=F32)


def dot_b(a, b):
    return lax.dot_general(a, b, (((1,), (1,)), ((), ())), preferred_element_type=F32)


def split2(v):
    hi = v.astype(BF16)
    return hi, (v - hi.astype(F32)).astype(BF16)


def dot3(ah, al, bh, bl):
    return dot_b(ah, bh) + (dot_b(ah, bl) + dot_b(al, bh))


def pack_kernel(dst_ref, tiles_ref, rows_ref, out_ref, stage, sems):
    step = pl.program_id(0)
    steps = pl.num_programs(0)
    slot = lax.rem(step, 2)
    per = tiles_ref.shape[0]

    def copy(at, i, which):
        return pltpu.make_async_copy(
            stage.at[which, i], out_ref.at[dst_ref[at * per + i]], sems.at[which, i])

    @pl.when(step >= 2)
    def _():
        for i in range(per):
            copy(step - 2, i, slot).wait()

    sub = lax.broadcasted_iota(jnp.int32, (TB, TB), 0)
    for i in range(per):
        pick = jnp.where(sub == rows_ref[i:i + 1, :], 1.0, 0.0).astype(BF16)
        tile = tiles_ref[i]
        hi = tile.astype(BF16)
        rest = tile - hi.astype(F32)
        mid = rest.astype(BF16)
        low = (rest - mid.astype(F32)).astype(BF16)
        moved = jnp.dot(pick, hi, preferred_element_type=F32)
        moved = moved + jnp.dot(pick, mid, preferred_element_type=F32)
        moved = moved + jnp.dot(pick, low, preferred_element_type=F32)
        stage[slot, i] = moved
    for i in range(per):
        copy(step, i, slot).start()

    @pl.when(step == steps - 1)
    def _():
        for i in range(per):
            copy(step - 1, i, 1 - slot).wait()
        for i in range(per):
            copy(step, i, slot).wait()


def pack(dst, tiles, rows, slots):
    count = tiles.shape[0]
    per = PER
    return pl.pallas_call(
        pack_kernel,
        grid_spec=pltpu.PrefetchScalarGridSpec(
            num_scalar_prefetch=1,
            grid=(count // per,),
            in_specs=[
                pl.BlockSpec((per, TB, TB), lambda i, d: (i, 0, 0)),
                pl.BlockSpec((per, TB), lambda i, d: (i, 0)),
            ],
            out_specs=pl.BlockSpec(memory_space=pl.ANY),
            scratch_shapes=[
                pltpu.VMEM((2, per, TB, TB), F32),
                pltpu.SemaphoreType.DMA((2, per)),
            ],
        ),
        out_shape=jax.ShapeDtypeStruct((slots, TB, TB), F32),
        name="pack",
    )(dst, tiles, rows)


def bcast_kernel(pa_ref, pc_ref, pt_ref, ga_ref, gc_ref, gr_ref, gt_ref,
                 s1a, s1c, r1a, r1c, loc, ss, rs, fs, fr, xs, xr):
    row = lax.axis_index("row")
    y = lax.axis_index("col")
    core = lax.rem(row, 2)
    z = lax.rem(lax.div(row, 2), 4)
    x = lax.div(row, 8)
    xz = lax.div(row, 2)
    pos = {"x": x, "y": y, "z": z}

    def device(axis, p):
        q = dict(pos)
        q[axis] = p
        return ((q["x"] * 4 + q["z"]) * 2 + core, q["y"])

    def remote(src, dst, send, recv, dev):
        return pltpu.make_async_remote_copy(
            src_ref=src, dst_ref=dst, send_sem=send, recv_sem=recv,
            device_id=dev, device_id_type=MESH)

    def piece_a(q):
        return pa_ref.at[:, q], ga_ref.at[:, y, core, lax.div(q, 4), lax.rem(q, 4)]

    def send_a(q):
        s, d = piece_a(q)
        return remote(s, d, s1a.at[q], r1a.at[0], (q * 2 + core, y))

    to_col = row - 2
    to_core = lax.div(y, 2)

    def piece_c(q):
        return pc_ref.at[q], gc_ref.at[y, lax.div(q, 4), lax.rem(q, 4)]

    def send_c(q):
        s, d = piece_c(q)
        return remote(s, d, s1c.at[q], r1c.at[lax.rem(y, 2)], (q * 2 + to_core, to_col))

    barrier = pltpu.get_barrier_semaphore()

    def greet(dev):
        pl.semaphore_signal(barrier, inc=1, device_id=dev, device_id_type=MESH)

    for axis in "xyz":
        for shift in (1, 3):
            greet(device(axis, lax.rem(pos[axis] + shift, 4)))
    greet((xz * 2 + (1 - core), y))

    is_a = row < 2
    is_c = (row >= 2) & (row < 6)

    def keeps(q):
        return (q == xz) & (to_core == core) & (to_col == y)

    def mine(h):
        return (2 * core + h == y) & (row == y + 2)

    @pl.when(is_a)
    def _():
        @pl.loop(1, 16)
        def _(q):
            greet((q * 2 + core, y))

    @pl.when(jnp.logical_not(is_a))
    def _():
        greet((core, y))

    @pl.when(is_c)
    def _():
        @pl.loop(0, 16)
        def _(q):
            @pl.when(jnp.logical_not(keeps(q)))
            def _():
                greet((q * 2 + to_core, to_col))

    for h in range(2):
        @pl.when(jnp.logical_not(mine(h)))
        def _():
            greet((y + 2, 2 * core + h))

    peers = 7 + jnp.where(is_a, 15, 1)
    peers = peers + jnp.where(is_c, jnp.where((to_core == core) & (to_col == y), 15, 16), 0)
    for h in range(2):
        peers = peers + jnp.where(mine(h), 0, 1)
    pl.semaphore_wait(barrier, peers)

    @pl.when(is_a)
    def _():
        s, d = piece_a(0)
        pltpu.make_async_copy(s, d, loc.at[0]).start()

        @pl.loop(1, 16)
        def _(q):
            send_a(q).start()

    @pl.when(is_c)
    def _():
        @pl.loop(0, 16)
        def _(q):
            @pl.when(keeps(q))
            def _():
                s, d = piece_c(q)
                pltpu.make_async_copy(s, d, loc.at[1]).start()

            @pl.when(jnp.logical_not(keeps(q)))
            def _():
                send_c(q).start()

    chains = []
    for s, order in enumerate(ORDERS):
        chains.append(("a", s, order))
    for s, order in enumerate((("z", "x"), ("x", "z"))):
        chains.append(("c", s, order))
    chains.append(("r", 0, ("y",)))
    chains.append(("t", 0, ("z", "x", "y")))
    shared = [n for n in range(len(chains)) if chains[n][0] != "r"]
    total = len(chains)

    def block(kind, s, order, t, p, half=None, cut=None):
        ind = {}
        for j, a in enumerate(order):
            ind[a] = slice(None) if j < t else (p if j == t else pos[a])
        if cut is not None and kind != "r":
            ind[order[0]] = cut
        if kind == "a":
            tail = () if half is None else (pl.ds(8 * half, 8), slice(None))
            fill = () if half is None else tail
            return ga_ref.at[(s, ind["y"], core, ind["x"], ind["z"]) + fill]
        if kind == "r":
            first, size = (0, 16) if half is None else (8 * half, 8)
            if cut is not None:
                size = size // 4
                first = first + cut * size
            return gr_ref.at[p, pl.ds(first, size)]
        if kind == "t":
            fill = () if half is None else (pl.ds(8 * half, 8), slice(None))
            return gt_ref.at[(ind["y"], core, ind["x"], ind["z"]) + fill]
        fill = () if half is None else (pl.ds(24 * half, 24), slice(None))
        return gc_ref.at[(2 * core + s, ind["x"], ind["z"]) + fill]

    sibling = (xz * 2 + (1 - core), y)

    def cuts(n, t):
        if chains[n][0] == "t":
            return (None,)
        return range(4) if t > 0 or chains[n][0] == "r" else (None,)

    def near(n, t, up, cut=None):
        kind, s, order = chains[n]
        a = order[t]
        p = pos[a]
        b = block(kind, s, order, t, p, None, cut)
        src = b
        if kind == "r":
            src = pc_ref if cut is None else pc_ref.at[pl.ds(cut * 4, 4)]
        return remote(src, b, ss.at[n, t, up], rs.at[n, t, up],
                      device(a, lax.rem(p + (1 if up else 3), 4)))

    def near_wait(n, t, up):
        kind, s, order = chains[n]
        a = order[t]
        b = block(kind, s, order, t, lax.rem(pos[a] + (3 if up else 1), 4))
        remote(b, b, ss.at[n, t, up], rs.at[n, t, up], (row, y)).wait_recv()

    def far(n, t, up, cut=None):
        kind, s, order = chains[n]
        a = order[t]
        p = pos[a]
        b = block(kind, s, order, t, lax.rem(p + (3 if up else 1), 4), 0 if up else 1, cut)
        return remote(b, b, fs.at[n, t, up], fr.at[n, t, up],
                      device(a, lax.rem(p + (1 if up else 3), 4)))

    def far_wait(n, t, up):
        kind, s, order = chains[n]
        a = order[t]
        b = block(kind, s, order, t, lax.rem(pos[a] + 2, 4), 0 if up else 1)
        remote(b, b, fs.at[n, t, up], fr.at[n, t, up], (row, y)).wait_recv()

    def cross(n, shift, cut=None):
        kind, s, order = chains[n]
        t = len(order) - 1
        b = block(kind, s, order, t, lax.rem(pos[order[t]] + shift, 4), None, cut)
        return remote(b, b, xs.at[n, shift], xr.at[n, shift], sibling)

    def cross_wait(n, shift):
        kind, s, order = chains[n]
        t = len(order) - 1
        ind = {}
        for j, a in enumerate(order):
            ind[a] = slice(None) if j < t else lax.rem(pos[a] + shift, 4)
        if kind == "a":
            b = ga_ref.at[s, ind["y"], 1 - core, ind["x"], ind["z"]]
        elif kind == "t":
            b = gt_ref.at[ind["y"], 1 - core, ind["x"], ind["z"]]
        else:
            b = gc_ref.at[2 * (1 - core) + s, ind["x"], ind["z"]]
        remote(b, b, xs.at[n, shift], xr.at[n, shift], (row, y)).wait_recv()

    diag, column, own = (6, 0, 1, 2), (3, 4), (5,)
    table = pltpu.make_async_copy(pt_ref, gt_ref.at[y, core, x, z], loc.at[2])
    table.start()
    for up in range(2):
        for cut in cuts(5, 0):
            near(5, 0, up, cut).start()
    @pl.when(is_a)
    def _():
        s, d = piece_a(0)
        pltpu.make_async_copy(s, d, loc.at[0]).wait()

    @pl.when(jnp.logical_not(is_a))
    def _():
        s = pa_ref.at[:, 0]
        remote(s, ga_ref.at[:, y, core, x, z], s1a.at[0], r1a.at[0], (row, y)).wait_recv()

    def share(n, shift):
        for cut in (None,) if chains[n][0] == "t" else range(4):
            cross(n, shift, cut).start()

    def begin(ns, t):
        for n in ns:
            for up in range(2):
                for cut in cuts(n, t):
                    near(n, t, up, cut).start()

    def forward(ns, t):
        for n in ns:
            for up in range(2):
                near_wait(n, t, up)
                for cut in cuts(n, t):
                    far(n, t, up, cut).start()
                if n in shared and t == len(chains[n][2]) - 1:
                    share(n, 3 if up else 1)

    def settle(n, t):
        for up in range(2):
            far_wait(n, t, up)

    def advance(ns, t):
        for n in ns:
            settle(n, t)
            begin([n], t + 1)
            if t + 1 == len(chains[n][2]) - 1:
                share(n, 0)

    def finish(ns, t):
        for n in ns:
            settle(n, t)
            share(n, 2)

    table.wait()
    begin(diag, 0)
    for h in range(2):
        yy = 2 * core + h

        @pl.when(mine(h))
        def _():
            s, d = piece_c(xz)
            pltpu.make_async_copy(s, d, loc.at[1]).wait()

        @pl.when(jnp.logical_not(mine(h)))
        def _():
            remote(pc_ref.at[0], gc_ref.at[yy, x, z], s1c.at[0], r1c.at[h], (row, y)).wait_recv()

    begin(column, 0)
    forward(diag, 0)
    forward(column, 0)
    advance(diag, 0)
    advance(column, 0)
    forward(own, 0)
    forward(diag, 1)
    forward(column, 1)
    advance(diag, 1)
    finish(column, 1)
    forward(diag, 2)
    finish(diag, 2)
    settle(5, 0)
    for n in shared:
        for shift in range(4):
            cross_wait(n, shift)
    for n in range(total):
        for t in range(len(chains[n][2])):
            for up in range(2):
                near(n, t, up).wait_send()
                far(n, t, up).wait_send()
    for n in shared:
        for shift in range(4):
            cross(n, shift).wait_send()

    @pl.when(is_a)
    def _():
        @pl.loop(1, 16)
        def _(q):
            send_a(q).wait_send()

    @pl.when(is_c)
    def _():
        @pl.loop(0, 16)
        def _(q):
            @pl.when(jnp.logical_not(keeps(q)))
            def _():
                send_c(q).wait_send()


def bcast(panel, table):
    rows, cols = panel.shape
    dma = pltpu.SemaphoreType.DMA
    return pl.pallas_call(
        bcast_kernel,
        in_specs=[pl.BlockSpec(memory_space=pl.ANY)] * 3,
        out_specs=[pl.BlockSpec(memory_space=pl.ANY)] * 4,
        out_shape=[
            jax.ShapeDtypeStruct((3, 4, 2, 4, 4, 16, cols), F32),
            jax.ShapeDtypeStruct((4, 4, 4, 48, cols), F32),
            jax.ShapeDtypeStruct((4, 16, 48, cols), F32),
            jax.ShapeDtypeStruct((4, 2, 4, 4) + table.shape, F32),
        ],
        scratch_shapes=[
            dma((16,)), dma((16,)), dma((1,)), dma((2,)), dma((3,)),
            dma((7, 3, 2)), dma((7, 3, 2)), dma((7, 3, 2)), dma((7, 3, 2)),
            dma((7, 4)), dma((7, 4)),
        ],
        compiler_params=pltpu.CompilerParams(has_side_effects=True, collective_id=0),
        name="bcast",
    )(panel.reshape(3, 16, 16, cols), panel.reshape(16, 48, cols), table)


def wide(v):
    return jnp.broadcast_to(v, (8, 128))


def small_inverse(cols):
    c = [[None] * 8 for _ in range(8)]
    for j in range(8):
        for i in range(j, 8):
            c[i][j] = wide(cols[j][i:i + 1, :])
    t = [[None] * 8 for _ in range(8)]
    for j in range(8):
        r = lax.rsqrt(c[j][j])
        t[j][j] = r
        for i in range(j + 1, 8):
            c[i][j] = c[i][j] * r
        for m in range(j + 1, 8):
            for i in range(m, 8):
                c[i][m] = c[i][m] - c[i][j] * c[m][j]
        for k in range(j):
            s = c[j][k] * t[k][k]
            for m in range(k + 1, j):
                s = s + c[j][m] * t[m][k]
            t[j][k] = -(s * r)
    return t


def factor_block(d):
    row = lax.broadcasted_iota(jnp.int32, (NB, NB), 0)
    col = lax.broadcasted_iota(jnp.int32, (NB, NB), 1)
    eye = jnp.where(row == col, 1.0, 0.0).astype(F32)
    groups = NB // 8
    r = [d[8 * g:8 * g + 8, :] for g in range(groups)]
    w = [eye[8 * g:8 * g + 8, :] for g in range(groups)]
    sub = lax.broadcasted_iota(jnp.int32, (8, NB), 0)
    us, vs = [], []
    for g in range(groups):
        cols = [wide(r[g][:, 8 * g + j:8 * g + j + 1]) for j in range(8)]
        t = small_inverse(cols)
        u = v = None
        for j in range(8):
            part = jnp.zeros((8, NB), F32)
            for i in range(j, 8):
                part = jnp.where(sub == i, t[i][j], part)
            du, dv = part * r[g][j:j + 1, :], part * w[g][j:j + 1, :]
            u, v = (du, dv) if u is None else (u + du, v + dv)
        us.append(u)
        vs.append(v)
        if g + 1 < groups:
            nxt = [wide(r[g + 1][:, 8 * g + j:8 * g + j + 1]) for j in range(8)]
            ra, wa = r[g + 1], w[g + 1]
            for j in range(8):
                m = nxt[0] * t[j][0]
                for k in range(1, j + 1):
                    m = m + nxt[k] * t[j][k]
                ra = ra - m * u[j:j + 1, :]
                wa = wa - m * v[j:j + 1, :]
            r[g + 1], w[g + 1] = ra, wa
        if g + 2 < groups:
            ut = jnp.transpose(u)
            for g2 in range(g + 2, groups):
                blk = ut[8 * g2:8 * g2 + 8, :]
                ra, wa = r[g2], w[g2]
                for j in range(8):
                    m = wide(blk[:, j:j + 1])
                    ra = ra - m * u[j:j + 1, :]
                    wa = wa - m * v[j:j + 1, :]
                r[g2], w[g2] = ra, wa
    upper = jnp.concatenate(us, axis=0)
    inverse = jnp.concatenate(vs, axis=0)
    return jnp.where(col >= row, upper, 0.0), inverse


def chol_kernel(ga_ref, l_ref, w_ref, c_ref):
    def at(i):
        if isinstance(i, int):
            return slice(i * NB, (i + 1) * NB)
        return pl.ds(pl.multiple_of(i * NB, NB), NB)

    def given(i, j):
        r, q = lax.rem(i, 6), lax.rem(i, 2)
        return ga_ref[lax.div(r, 2), lax.div(j, 3), lax.div(i, 6), at(q), at(lax.rem(j, 3))]

    def sym(i, j):
        return 0.5 * (given(i, j) + given(j, i).T)

    l_ref[...] = jnp.zeros_like(l_ref)
    w_ref[...] = jnp.zeros_like(w_ref)
    c_ref[...] = jnp.zeros_like(c_ref)
    d = sym(jnp.int32(0), jnp.int32(0))
    per = 4
    for stage in range(KB // per):
        top = stage * per
        below = slice(top * NB, PW)
        known = slice(0, (top + per) * NB)
        index = top * NB + lax.broadcasted_iota(jnp.int32, (PW - top * NB, NB), 0)

        def step(k, d):
            last = jnp.maximum(k - 1, 0)
            after = jnp.minimum(k + 1, KB - 1)
            column = dot_nt(c_ref[below, :], w_ref[at(last), :])
            fresh = (index >= k * NB) & (k > 0)
            l_ref[below, at(last)] = jnp.where(fresh, column, l_ref[below, at(last)])
            acc = dot_nt(l_ref[below, known], l_ref[at(k), known])
            for i in range(top, KB):
                c_ref[at(i), :] = sym(jnp.int32(i), k) - acc[at(i - top), :]
            row = l_ref[at(after), known]
            rest = sym(after, after) - dot_nt(row, row)

            upper, inverse = factor_block(d)
            w_ref[at(k), :] = inverse
            nxt = dot_nt(c_ref[at(after), :], inverse)
            l_ref[at(after), at(k)] = nxt
            l_ref[at(k), at(k)] = upper.T
            return rest - dot_nt(nxt, nxt)

        d = lax.fori_loop(top, top + per, step, d)


def chol(ga):
    return pl.pallas_call(
        chol_kernel,
        out_shape=[
            jax.ShapeDtypeStruct((PW, PW), F32),
            jax.ShapeDtypeStruct((PW, NB), F32),
        ],
        scratch_shapes=[pltpu.VMEM((PW, NB), F32)],
        compiler_params=pltpu.CompilerParams(vmem_limit_bytes=BIG),
        cost_estimate=pl.CostEstimate(
            flops=60_000_000_000, bytes_accessed=20_000_000, transcendentals=0),
        name="chol",
    )(ga)


def solve_kernel(place_ref, l_ref, w_ref, own_ref, pr_ref, pc_ref, t_ref, f_ref, o_ref,
                 lh, ll, wh, wl, xh, xl, keep):
    row = place_ref[0]
    col = place_ref[1]
    rows = pr_ref.shape[1]
    wide_cols = pr_ref.shape[2]
    nb = 2 * NB

    @pl.loop(0, KB)
    def _(k):
        at = pl.ds(pl.multiple_of(k * NB, NB), NB)
        hi, lo = split2(l_ref[at, :])
        lh[at, :] = hi
        ll[at, :] = lo

    for k in range(KB // 2):
        a, b = 2 * k * NB, (2 * k + 1) * NB
        w1, w2 = w_ref[a:a + NB, :], w_ref[b:b + NB, :]
        cross = l_ref[b:b + NB, a:a + NB]
        mid = jnp.dot(cross, w1, precision=lax.Precision.HIGHEST, preferred_element_type=F32)
        low = -jnp.dot(w2, mid, precision=lax.Precision.HIGHEST, preferred_element_type=F32)
        zero = jnp.zeros((NB, NB), F32)
        hi, lo = split2(jnp.concatenate(
            [jnp.concatenate([w1, zero], axis=1), jnp.concatenate([low, w2], axis=1)], axis=0))
        wh[k] = hi
        wl[k] = lo

    half = rows // 2
    for part, src in enumerate((pr_ref, pc_ref)):
        @pl.loop(0, 2)
        def _(g):
            band = pl.ds(pl.multiple_of(g * half, NB), half)
            for k in range(KB // 2):
                cols = []
                for h in range(2):
                    at = (2 * k + h) * NB
                    j, cut = at // wide_cols, slice(at % wide_cols, at % wide_cols + NB)
                    piece = src[j, band, cut]
                    if part == 0:
                        piece = jnp.where(col == j, own_ref[band, cut], piece)
                    cols.append(piece)
                v = jnp.concatenate(cols, axis=1)
                here = slice(k * nb, (k + 1) * nb)
                if k > 0:
                    done = slice(0, k * nb)
                    v = v - dot3(xh[part, band, done], xl[part, band, done],
                                 lh[here, done], ll[here, done])
                vh, vl = split2(v)
                v = dot3(vh, vl, wh[k], wl[k])
                hi, lo = split2(v)
                xh[part, band, here] = hi
                xl[part, band, here] = lo
                if part == 0:
                    for h in range(2):
                        at = (2 * k + h) * NB
                        keep[at // wide_cols, band, at % wide_cols:at % wide_cols + NB] = (
                            v[:, h * NB:(h + 1) * NB])

    @pl.when(row >= 2)
    def _():
        f_ref[...] = keep[col]

        @pl.loop(0, rows // 256)
        def _(i):
            at = pl.ds(pl.multiple_of(i * 256, 256), 256)
            o_ref[at, :] = t_ref[at, :] - dot3(xh[0, at, :], xl[0, at, :], xh[1], xl[1])

    @pl.when(row < 2)
    def _():
        first = pl.ds(pl.multiple_of(row * rows, NB), rows)
        f_ref[...] = l_ref[first, pl.ds(pl.multiple_of(col * wide_cols, NB), wide_cols)]
        o_ref[...] = t_ref[...]


def solve(place, factor, inverse, own, mine, theirs, trailing):
    n, rows, cols = mine.shape
    smem = pl.BlockSpec(memory_space=pltpu.SMEM)
    vmem = pl.BlockSpec(memory_space=pltpu.VMEM)
    return pl.pallas_call(
        solve_kernel,
        in_specs=[smem] + [vmem] * 6,
        out_specs=[vmem, vmem],
        out_shape=[
            jax.ShapeDtypeStruct((rows, cols), F32),
            jax.ShapeDtypeStruct(trailing.shape, F32),
        ],
        scratch_shapes=[
            pltpu.VMEM((PW, PW), BF16), pltpu.VMEM((PW, PW), BF16),
            pltpu.VMEM((KB // 2, 2 * NB, 2 * NB), BF16), pltpu.VMEM((KB // 2, 2 * NB, 2 * NB), BF16),
            pltpu.VMEM((2, rows, PW), BF16), pltpu.VMEM((2, rows, PW), BF16),
            pltpu.VMEM((n, rows, cols), F32),
        ],
        compiler_params=pltpu.CompilerParams(vmem_limit_bytes=BIG),
        cost_estimate=pl.CostEstimate(
            flops=30_000_000_000, bytes_accessed=30_000_000, transcendentals=0),
        name="solve",
    )(place, factor, inverse, own, mine, theirs, trailing)


def add_kernel(target_ref, *refs):
    *tile_refs, base_ref, out_ref, total = refs
    step = pl.program_id(0)
    streams = len(tile_refs)
    per = streams * tile_refs[0].shape[0]
    rows = out_ref.shape[0]
    tile_cols = out_ref.shape[1] // TB

    @pl.when(step == 0)
    def _():
        total[0:rows, :] = base_ref[...]

    spare = (rows // TB) * tile_cols
    for i in range(per):
        sizes = per // streams
        at = (i % streams) * (pl.num_programs(0) * sizes) + step * sizes + i // streams
        target = target_ref[at]
        target = jnp.where(target < 0, spare, target)
        r = pl.ds(pl.multiple_of(lax.div(target, tile_cols) * TB, TB), TB)
        c = pl.ds(pl.multiple_of(lax.rem(target, tile_cols) * TB, TB), TB)
        total[r, c] = total[r, c] + tile_refs[i % streams][i // streams]

    @pl.when(step == pl.num_programs(0) - 1)
    def _():
        out_ref[...] = total[0:rows, :]


def stream_block(first, i, t):
    return (first + i, 0, 0)


def extend_add(target, tiles, base):
    streams, size = 4, 8
    steps = tiles.shape[0] // (streams * size)
    return pl.pallas_call(
        add_kernel,
        grid_spec=pltpu.PrefetchScalarGridSpec(
            num_scalar_prefetch=1,
            grid=(steps,),
            in_specs=[
                pl.BlockSpec((size, TB, TB), functools.partial(stream_block, s * steps))
                for s in range(streams)
            ] + [
                pl.BlockSpec(base.shape, lambda i, t: (0, 0)),
            ],
            out_specs=pl.BlockSpec(base.shape, lambda i, t: (0, 0)),
            scratch_shapes=[pltpu.VMEM((base.shape[0] + TB, base.shape[1]), F32)],
        ),
        out_shape=jax.ShapeDtypeStruct(base.shape, F32),
        compiler_params=pltpu.CompilerParams(vmem_limit_bytes=40 << 20),
        name="extend_add",
    )(target, *([tiles] * streams), base)


def body(panel, trailing, child_tiles, child_owner, child_tile, child_rows):
    devices = lax.axis_size("row") * lax.axis_size("col")
    count = child_owner.shape[0]
    cap = 2
    both = ("row", "col")
    order = jnp.arange(count, dtype=jnp.int32)
    same = child_owner[:, None] == child_owner[None, :]
    rank = jnp.sum(jnp.where(same & (order[None, :] < order[:, None]), 1, 0), axis=1)
    dst = (child_owner * cap + rank).astype(jnp.int32)
    slots = devices * cap
    hit = dst[:, None] == jnp.arange(slots, dtype=jnp.int32)[None, :]
    target = (jnp.sum(jnp.where(hit, child_tile[:, None] + 1, 0), axis=0) - 1).astype(jnp.int32)
    table = jnp.pad(target.reshape(devices, cap).T.astype(F32), ((0, 14), (0, 0)))
    packed = pack(dst, child_tiles, child_rows, slots)
    ga, gc, mine, tables = bcast(panel, table)
    packed, ga = lax.optimization_barrier((packed, ga))
    got = lax.all_to_all(
        packed.reshape(devices, cap, TB, TB), both, split_axis=0, concat_axis=0, tiled=True)
    row_index, col_index = lax.axis_index("row"), lax.axis_index("col")
    me = row_index * lax.axis_size("col") + col_index
    lane = jnp.arange(devices, dtype=jnp.int32)
    picked = jnp.sum(jnp.where(lane == me, tables[..., :cap, :], 0.0), axis=-1)
    got_target = picked.transpose(2, 3, 1, 0, 4).astype(jnp.int32)
    factor, inverse = chol(ga.reshape(3, 4, 2, 256, panel.shape[1]))
    place = jnp.stack([row_index, col_index]).astype(jnp.int32)
    factor_panel, base = solve(
        place, factor, inverse, panel, mine.reshape(4, *panel.shape), gc.reshape(4, *panel.shape), trailing)
    new_trailing = extend_add(got_target.reshape(-1), got.reshape(-1, TB, TB), base)
    return factor_panel, new_trailing


def solution(mesh):
    in_specs = (
        P("row", "col"),
        P("row", "col"),
        P(("row", "col"), None, None),
        P(("row", "col")),
        P(("row", "col")),
        P(("row", "col"), None),
    )
    out_specs = (P("row", "col"), P("row", "col"))
    return jax.shard_map(body, mesh=mesh, in_specs=in_specs, out_specs=out_specs, check_vma=False)
```
